32 devices in a mesh: row: 4 (over y, core), blk: 8 (over z, x).
Axes of the slice: x: 2, y: 2, z: 4, core: 2. Of those that a mesh axis runs over, the one named last changes fastest.
Arguments:
- right_side: float32 [4, 8, 8, 32, 256], P('row', 'blk')
- noise_level: float32 [4, 8, 8, 256], P('row', 'blk'), may hold values from 3 to 6
- near_blocks: bfloat16 [4, 8, 8, 9, 256, 256], P('row', 'blk'), as said below
- skeleton_basis: bfloat16 [4, 8, 8, 64, 256], P('row', 'blk'), may hold values from -0.125 to 0.125
- skeleton_index: int32 [4, 8, 64], P('row', 'blk'), may hold values from 0 to 2047, as said below
- far_list: int32 [4, 8, 7], P('row', 'blk'), may hold values from 0 to 7, as said below
- couplings: bfloat16 [4, 8, 7, 64, 64], P('row', 'blk'), as said below
Outputs:
- solution: float32 [4, 8, 8, 32, 256], P('row', 'blk')
- residual: float32 [4, 8, 8, 32, 256], P('row', 'blk')
- quadratic: float32 [32], replicated
The draws below stay inside these ranges and needn't reach their ends.
Inputs may be any that keep to these rules, and one draw needn't show every extreme that they name: `far_list`: each device's 7 entries are distinct, none is the device's own blk index, and the two cyclic neighbours along blk are always among them; box b lists box b' exactly when b' lists b, and within a row every box's far boxes lie at the same set of cyclic offsets from its own index. `couplings`: the coupling that box b holds for far box b' is the transpose of the one that b' holds for b. `near_blocks`: A leaf's block for near slot s is the transpose of the block that its slot-s neighbour holds for slot 8 - s; slot 4 blocks are symmetric. `skeleton_index`: each device's 64 entries are distinct tracers of its 2048.
All inputs are finite; a program needn't handle non-finite values.
Results may differ from the reference program's by a relative error of at most 0.03.
Values may be sent and summed in bfloat16 or wider, within the bound.
A program may use at most 64 MiB of HBM per device.

```python
import math
import jax
import jax.numpy as jnp

LEAF = 256
SKEL = 64
RHS = 32
NEAR = 9
ITERS = 4
LEAF_ROWS = 2
LEAF_COLS = 4
LEAF_DEV = 8
FAR = 7
POINTS = 65536
N_ROW = 4
N_BLK = 8


def draw_right_side(key, part):
    first_key, second_key = jax.random.split(key, 2)
    shape = (N_ROW, N_BLK, LEAF_DEV, RHS, LEAF)
    device_count = N_ROW * N_BLK
    device_order = jnp.arange(device_count, dtype=jnp.float32).reshape(N_ROW, N_BLK)
    device_ramp = 3.0 ** (device_order / (device_count - 1))
    column_scale = jnp.exp(jax.random.uniform(second_key, (RHS,), jnp.float32, math.log(0.3), math.log(3.0)))
    base = jax.random.normal(first_key, shape, jnp.float32)
    return base * device_ramp[:, :, None, None, None] * column_scale[None, None, None, :, None]


def draw_near_blocks(key, part):
    grid_rows = N_ROW * LEAF_ROWS
    grid_cols = N_BLK * LEAF_COLS
    scale = 4.0 * (8.0 * NEAR * LEAF) ** (-0.5)
    shape = (grid_rows, grid_cols, LEAF, LEAF)
    own = jax.random.normal(jax.random.fold_in(key, 41), shape, jnp.float32)
    own = (own + jnp.swapaxes(own, -1, -2)) * 0.70710678 * scale
    own = own + 3.0 * jnp.eye(LEAF, dtype=jnp.float32)[None, None, :, :]
    slots = [own] * 9
    forward = ((5, 0, 1), (6, 1, -1), (7, 1, 0), (8, 1, 1))
    for slot_index, step_row, step_col in forward:
        block = jax.random.normal(jax.random.fold_in(key, 50 + slot_index), shape, jnp.float32) * scale
        slots[slot_index] = block
        slots[8 - slot_index] = jnp.swapaxes(jnp.roll(block, (step_row, step_col), axis=(0, 1)), -1, -2)
    stacked = jnp.stack(slots, axis=2)
    stacked = stacked.reshape(N_ROW, LEAF_ROWS, N_BLK, LEAF_COLS, NEAR, LEAF, LEAF)
    stacked = jnp.moveaxis(stacked, 2, 1)
    return stacked.reshape(N_ROW, N_BLK, LEAF_ROWS * LEAF_COLS, NEAR, LEAF, LEAF).astype(jnp.bfloat16)


def draw_skeleton_index(key, part):
    points = LEAF_DEV * LEAF
    scores = jax.random.randint(jax.random.fold_in(key, 11), (N_ROW, N_BLK, points), 0, 2 ** 30 // points)
    scores = scores * points + jnp.arange(points, dtype=jnp.int32)[None, None, :]
    ordering = jnp.argsort(scores, axis=-1)
    return ordering[:, :, :SKEL].astype(jnp.int32)


def far_structure(key):
    half = N_BLK // 2
    pairs = (FAR - 1) // 2
    candidates = max(half - 2, 1)
    scores = jax.random.randint(jax.random.fold_in(key, 23), (N_ROW, candidates), 0, 2 ** 30 // candidates)
    scores = scores * candidates + jnp.arange(candidates, dtype=jnp.int32)[None, :]
    drawn = (2 + jnp.argsort(scores, axis=-1)[:, :pairs - 1]).astype(jnp.int32)
    nearest = jnp.ones((N_ROW, 1), jnp.int32)
    chosen = jnp.concatenate([nearest, drawn], axis=1).astype(jnp.int32)
    middle = jnp.full((N_ROW, 1), half, jnp.int32)
    offsets = jnp.concatenate([chosen, middle, N_BLK - chosen], axis=1).astype(jnp.int32)
    order_scores = jax.random.randint(jax.random.fold_in(key, 29), (N_ROW, N_BLK, FAR), 0, 2 ** 30 // FAR)
    order_scores = order_scores * FAR + jnp.arange(FAR, dtype=jnp.int32)[None, None, :]
    ordering = jnp.argsort(order_scores, axis=-1).astype(jnp.int32)
    return (offsets, ordering)


def draw_far_list(key, part):
    offsets, ordering = far_structure(key)
    row_index = jnp.arange(N_ROW, dtype=jnp.int32)[:, None, None]
    picked = offsets[row_index, ordering]
    own_index = jnp.arange(N_BLK, dtype=jnp.int32)[None, :, None]
    return ((own_index + picked) % N_BLK).astype(jnp.int32)


def draw_couplings(key, part):
    offsets, ordering = far_structure(key)
    half = N_BLK // 2
    pairs = (FAR - 1) // 2
    scale = 1.5 * (8.0 * FAR * SKEL) ** (-0.5)
    base = jax.random.normal(jax.random.fold_in(key, 31), (N_ROW, N_BLK, pairs + 1, SKEL, SKEL), jnp.float32) * scale
    positive = base[:, :, :pairs]
    centre = base[:, :, pairs]
    lower = jnp.arange(N_BLK, dtype=jnp.int32)[None, :, None, None] < half
    centre = jnp.where(lower, centre, jnp.swapaxes(jnp.roll(centre, half, axis=1), -1, -2))
    row_index = jnp.arange(N_ROW, dtype=jnp.int32)[:, None, None]
    partner = (jnp.arange(N_BLK, dtype=jnp.int32)[None, :, None] - offsets[:, None, :pairs]) % N_BLK
    pair_index = jnp.arange(pairs, dtype=jnp.int32)[None, None, :]
    negative = jnp.swapaxes(positive[row_index, partner, pair_index], -1, -2)
    canonical = jnp.concatenate([positive, centre[:, :, None], negative], axis=2)
    blk_index = jnp.arange(N_BLK, dtype=jnp.int32)[None, :, None]
    return canonical[row_index, blk_index, ordering].astype(jnp.bfloat16)


def shard_levels(key, shape, pieces, low, top_value):
    loudness, own = 1.0, jax.random.fold_in(key, 6)
    for dim, blocks in pieces:
        draws = jnp.exp(jax.random.uniform(jax.random.fold_in(own, dim), (blocks,), jnp.float32, low / len(pieces), top_value / len(pieces)))
        loudness = loudness * jnp.repeat(draws, shape[dim] // blocks).reshape([-1 if axis == dim else 1 for axis in range(len(shape))])
    return loudness


def normal_values(rng, dims, scale, reach, cuts=(), kind=jnp.bfloat16):
    entries = scale * jax.random.normal(rng, dims, jnp.float32)
    if cuts:
        entries = entries * shard_levels(rng, dims, cuts, -0.22, 0.18)
    return jnp.clip(entries, -reach, reach).astype(kind)


def setup_inputs(seed: int = 0) -> dict:
    seeds = jax.random.split(jax.random.key(seed), 8)
    return {
        "right_side": draw_right_side(jax.random.fold_in(seeds[7], 71), 0),
        "noise_level": jnp.clip(jnp.exp(math.log(6.0) - 0.6931472 * jax.random.uniform(seeds[1], (N_ROW, N_BLK, LEAF_DEV, LEAF), jnp.float32) ** shard_levels(seeds[1], (N_ROW, N_BLK, LEAF_DEV, LEAF), ((0, 4), (1, 8)), -0.2, 0.2)), 3.0, 6.0),
        "near_blocks": draw_near_blocks(jax.random.fold_in(seeds[7], 71), 0),
        "skeleton_basis": normal_values(seeds[3], (N_ROW, N_BLK, LEAF_DEV, SKEL, LEAF), (LEAF_DEV * LEAF) ** -0.5, 0.125, ((0, 4), (1, 8))),
        "skeleton_index": draw_skeleton_index(jax.random.fold_in(seeds[7], 71), 0),
        "far_list": draw_far_list(jax.random.fold_in(seeds[7], 71), 0),
        "couplings": draw_couplings(jax.random.fold_in(seeds[7], 71), 0),
    }


def to_grid(values):
    rest = values.shape[3:]
    shaped = values.reshape((N_ROW, N_BLK, LEAF_ROWS, LEAF_COLS) + rest)
    shaped = jnp.moveaxis(shaped, 2, 1)
    return shaped.reshape((N_ROW * LEAF_ROWS, N_BLK * LEAF_COLS) + rest)


def from_grid(values):
    rest = values.shape[2:]
    shaped = values.reshape((N_ROW, LEAF_ROWS, N_BLK, LEAF_COLS) + rest)
    shaped = jnp.moveaxis(shaped, 1, 2)
    return shaped.reshape((N_ROW, N_BLK, LEAF_ROWS * LEAF_COLS) + rest)


def skeleton_weights(rounded_dev, basis_dev, skeleton_dev):
    points = rounded_dev.shape[2]
    owner_leaf = skeleton_dev // points
    owner_point = skeleton_dev % points
    picked = rounded_dev[owner_leaf, :, owner_point].astype(jnp.float32)
    spread = jnp.einsum('lci,lki->ck', rounded_dev.astype(jnp.float32), basis_dev.astype(jnp.float32))
    return picked.T + spread


def spread_far(far_sum, basis_dev, skeleton_dev):
    points = basis_dev.shape[2]
    owner_leaf = skeleton_dev // points
    owner_point = skeleton_dev % points
    far_rounded = far_sum.astype(jnp.bfloat16).astype(jnp.float32)
    result = jnp.einsum('ck,lki->lci', far_rounded, basis_dev.astype(jnp.float32))
    return result.at[owner_leaf, :, owner_point].add(far_sum.T)


def apply_operator(direction, noise_level, grid_blocks, skeleton_basis, skeleton_index, far_list, couplings):
    rounded = direction.astype(jnp.bfloat16)
    n_rows = rounded.shape[0]
    field = to_grid(rounded)
    near = jnp.zeros(field.shape, jnp.float32)
    for slot_index in range(9):
        shift_row = 1 - slot_index // 3
        shift_col = 1 - slot_index % 3
        sources = jnp.roll(field, (shift_row, shift_col), axis=(0, 1))
        near = near + jnp.einsum('xyci,xyij->xycj', sources.astype(jnp.float32), grid_blocks[:, :, slot_index].astype(jnp.float32))
    result = from_grid(near)
    skeleton = jax.vmap(jax.vmap(skeleton_weights))(rounded, skeleton_basis, skeleton_index)
    skeleton_rounded = skeleton.astype(jnp.bfloat16)
    selected = skeleton_rounded[jnp.arange(n_rows)[:, None, None], far_list]
    far_sum = jnp.einsum('rbjck,rbjkm->rbcm', selected.astype(jnp.float32), couplings.astype(jnp.float32))
    result = result + jax.vmap(jax.vmap(spread_far))(far_sum, skeleton_basis, skeleton_index)
    return noise_level[:, :, :, None, :] * direction + result


def reference(right_side, noise_level, near_blocks, skeleton_basis, skeleton_index, far_list, couplings):
    grid_blocks = to_grid(near_blocks)

    def operate(field):
        return apply_operator(field, noise_level, grid_blocks, skeleton_basis, skeleton_index, far_list, couplings)

    axes = (0, 1, 2, 4)
    solution = jnp.zeros_like(right_side)
    residual = right_side
    direction = right_side
    norm_now = jnp.sum(residual * residual, axis=axes)
    for step_index in range(ITERS):
        applied = operate(direction)
        step_size = norm_now / jnp.sum(direction * applied, axis=axes)
        solution = solution + step_size[:, None] * direction
        residual = residual - step_size[:, None] * applied
        norm_next = jnp.sum(residual * residual, axis=axes)
        direction = residual + (norm_next / norm_now)[:, None] * direction
        norm_now = norm_next
    quadratic = jnp.sum(right_side * solution, axis=axes) / POINTS
    return solution, residual, quadratic
```

```python
import functools

import jax
import jax.numpy as jnp
from jax import lax
from jax.experimental import pallas as pl
from jax.experimental.pallas import tpu as pltpu
from jax.sharding import PartitionSpec as P

LEAF_ROWS = 2
LEAF_COLS = 4
APPLIES = 4
OWN = 4
MESH = pl.DeviceIdType.MESH
SHIFTS = ((0, -1), (0, 1), (-1, -1), (-1, 1), (1, -1), (1, 1), (-1, 0), (1, 0))
SHIFT_SUM, GRAM_SUM, LAST_SUM = range(3)
SUM_LANES = (128, 384, 128)
PAIRS = tuple((i, j) for i in range(APPLIES) for j in range(i + 1))


def span(shift, count, incoming):
    if shift == 0:
        return 1, count
    if incoming:
        return (0 if shift > 0 else count + 1), 1
    return (count if shift > 0 else 1), 1


def each(count, body):
    if count <= 32:
        for i in range(count):
            body(i)
    else:
        pl.loop(0, count)(body)


def plan(gram, shift, columns):
    def inner(u, v):
        terms = {}
        for i, a in enumerate(u):
            for j, b in enumerate(v):
                key = (max(i, j), min(i, j))
                terms[key] = a * b + terms[key] if key in terms else a * b
        total = None
        for key, value in terms.items():
            term = value * gram[key]
            total = term if total is None else total + term
        return total

    def apply(u):
        out = [shift * u[0]]
        for j in range(1, len(u)):
            out.append(u[j - 1] + shift * u[j])
        return out + [u[-1]]

    one = jnp.ones((1, columns), jnp.float32)
    zero = jnp.zeros((1, columns), jnp.float32)
    x, r, p = [], [one], [one]
    norm = gram[0, 0]
    for _ in range(APPLIES - 1):
        q = apply(p)
        step = norm / inner(p, q)
        x = [a + step * b for a, b in zip(x + [zero], p)]
        r = [a - step * b for a, b in zip(r + [zero], q)]
        norm_next = inner(r, r)
        turn = norm_next / norm
        p = [a + turn * b for a, b in zip(r, p + [zero])]
        norm = norm_next
    return x, r, p, norm


def kernel(
    n_row, n_blk, tracers,
    right_hbm, noise_hbm, blocks_hbm, basis_hbm, index_ref, far_ref, coupling_hbm,
    solution_out, residual_out, quadratic_out,
    vectors, noise_ref, coupling_ref, blocks, mixed, extended, applied, ahead, skel_0, skel_1, skel_2, skel_3,
    row_shift, row_gram, row_last, blk_shift, blk_gram, blk_last, quadratic_ref,
    first_sem, own_sem, load_sem, halo_send, halo_recv, skel_send, skel_recv,
    row_send, row_recv, blk_send, blk_recv, out_sem,
):
    leaves, columns, width = vectors.shape[1:]
    rank = basis_hbm.shape[1]
    far_count = coupling_ref.shape[0]
    my_row, my_blk = lax.axis_index("row"), lax.axis_index("blk")
    skeletons = (skel_0, skel_1, skel_2, skel_3)
    row_sums, blk_sums = (row_shift, row_gram, row_last), (blk_shift, blk_gram, blk_last)
    x_ref, r_ref, p_ref, u_ref = (ahead.at[i] for i in range(4))

    firsts = [
        pltpu.make_async_copy(source, target, first_sem.at[i])
        for i, (source, target) in enumerate((
            (right_hbm, vectors.at[0]),
            (basis_hbm, mixed.at[:, pl.ds(0, rank)]),
            (noise_hbm, noise_ref),
            (coupling_hbm, coupling_ref),
        ))
    ]
    own_load = pltpu.make_async_copy(blocks_hbm.at[:, OWN], blocks.at[:, OWN], own_sem)
    loads = []
    for l in range(leaves):
        for h, part in enumerate((pl.ds(0, OWN), pl.ds(OWN + 1, 8 - OWN))):
            loads.append(pltpu.make_async_copy(blocks_hbm.at[l, part], blocks.at[l, part], load_sem.at[l, h]))
    firsts[0].start()
    firsts[1].start()
    firsts[2].start()
    own_load.start()
    firsts[3].start()
    for load in loads:
        load.start()

    def row_at(o):
        return lax.rem(my_row + (o + n_row), n_row)

    def blk_at(o):
        return lax.rem(my_blk + (o + n_blk), n_blk)

    barrier = pltpu.get_barrier_semaphore()

    def greet(row, blk):
        pl.semaphore_signal(barrier, inc=1, device_id={"row": row, "blk": blk}, device_id_type=MESH)

    corners = [(dr, dc) for dr, dc in SHIFTS if dr and dc]
    for dr, dc in corners:
        greet(row_at(dr), blk_at(dc))
    each(n_row - 1, lambda i: greet(row_at(i + 1), my_blk))
    each(n_blk - 1, lambda i: greet(my_row, blk_at(i + 1)))
    greeted = len(corners) + n_row - 1 + n_blk - 1

    def halo(k, n):
        dr, dc = SHIFTS[n]
        (sr, nr), (sc, nc) = span(dr, LEAF_ROWS, False), span(dc, LEAF_COLS, False)
        (tr, _), (tc, _) = span(dr, LEAF_ROWS, True), span(dc, LEAF_COLS, True)
        return pltpu.make_async_remote_copy(
            src_ref=extended.at[k, pl.ds(sr, nr), pl.ds(sc, nc)],
            dst_ref=extended.at[k, pl.ds(tr, nr), pl.ds(tc, nc)],
            send_sem=halo_send.at[k, n],
            recv_sem=halo_recv.at[k, n],
            device_id={"row": row_at(dr), "blk": blk_at(dc)},
            device_id_type=MESH,
        )

    def row_copy(n, i):
        return pltpu.make_async_remote_copy(
            src_ref=row_sums[n].at[my_row],
            dst_ref=row_sums[n].at[my_row],
            send_sem=row_send.at[n],
            recv_sem=row_recv.at[n],
            device_id={"row": row_at(i + 1), "blk": my_blk},
            device_id_type=MESH,
        )

    def blk_copy(n, i):
        return pltpu.make_async_remote_copy(
            src_ref=blk_sums[n].at[my_blk],
            dst_ref=blk_sums[n].at[my_blk],
            send_sem=blk_send.at[n],
            recv_sem=blk_recv.at[n],
            device_id={"row": my_row, "blk": blk_at(i + 1)},
            device_id_type=MESH,
        )

    def skeleton_copy(k, i):
        return pltpu.make_async_remote_copy(
            src_ref=skeletons[k].at[my_blk],
            dst_ref=skeletons[k].at[my_blk],
            send_sem=skel_send.at[k],
            recv_sem=skel_recv.at[k],
            device_id={"row": my_row, "blk": blk_at(i + 1)},
            device_id_type=MESH,
        )

    def all_wait(every, sem):
        pltpu.make_async_copy(every, every, sem).wait()

    def sum_start(n, sums):
        whole = jnp.concatenate(sums, axis=0)
        rest = SUM_LANES[n] - whole.shape[0]
        if rest:
            whole = jnp.concatenate([whole, jnp.zeros((rest, 128), jnp.float32)], axis=0)
        high = whole.astype(jnp.bfloat16)
        left = whole - high.astype(jnp.float32)
        middle = left.astype(jnp.bfloat16)
        low = (left - middle.astype(jnp.float32)).astype(jnp.bfloat16)
        lines = lax.dot_general(
            jnp.ones((8, 3 * 128), jnp.bfloat16), jnp.concatenate([high, middle, low], axis=1),
            (((1,), (1,)), ((), ())), preferred_element_type=jnp.float32,
        )
        row_sums[n][my_row] = lines[:1]
        each(n_row - 1, lambda i: row_copy(n, i).start())

    def sum_next(n):
        all_wait(row_sums[n].at[pl.ds(0, n_row - 1)], row_recv.at[n])
        blk_sums[n][my_blk] = jnp.sum(row_sums[n][...], axis=0)
        each(n_blk - 1, lambda i: blk_copy(n, i).start())

    def sum_end(n):
        all_wait(blk_sums[n].at[pl.ds(0, n_blk - 1)], blk_recv.at[n])
        return jnp.sum(blk_sums[n][...], axis=0)

    spread_row = lax.broadcasted_iota(jnp.int32, (columns, columns), 0)
    spread_lane = lax.broadcasted_iota(jnp.int32, (columns, columns), 1)

    def per_column(line):
        wide = jnp.broadcast_to(line, (columns, columns))
        kept = jnp.where(spread_row == spread_lane, wide, 0.0)
        return jnp.sum(kept, axis=1, keepdims=True)

    def halves(product):
        total = product[:, :128]
        for h in range(1, width // 128):
            total = total + product[:, 128 * h : 128 * (h + 1)]
        return total

    def at(l):
        a, c = divmod(l, LEAF_COLS)
        return a + 1, c + 1

    def slots(l):
        a, c = divmod(l, LEAF_COLS)
        for s in range(9):
            if s != OWN:
                yield s, a + s // 3, c + s % 3

    def inside(row, col):
        return 1 <= row <= LEAF_ROWS and 1 <= col <= LEAF_COLS

    def publish(k, l, value):
        row, col = at(l)
        extended[k, row, col] = value.astype(jnp.bfloat16)

    def send_halos(k):
        for n in range(len(SHIFTS)):
            halo(k, n).start()

    def send_skeleton(k):
        both = jnp.zeros((columns, 2 * rank), jnp.float32)
        for l in range(leaves):
            both = both + lax.dot_general(
                extended[(k, *at(l))], mixed[l, : 2 * rank], (((1,), (1,)), ((), ())),
                preferred_element_type=jnp.float32,
            )
        skeletons[k][my_blk] = (both[:, :rank] + both[:, rank:]).astype(jnp.bfloat16)
        each(n_blk - 1, lambda i: skeleton_copy(k, i).start())

    def own_part(k, l):
        value = vectors[k, l]
        high = extended[(k, *at(l))]
        low = (value - high.astype(jnp.float32)).astype(jnp.bfloat16)
        product = jnp.dot(high, blocks[l, OWN], preferred_element_type=jnp.float32)
        product = product + jnp.dot(low, blocks[l, OWN], preferred_element_type=jnp.float32)
        return noise_ref[l : l + 1] * value + product

    def near_part(k, l, within):
        total = None
        for s, row, col in slots(l):
            if inside(row, col) == within:
                term = jnp.dot(extended[k, row, col], blocks[l, s], preferred_element_type=jnp.float32)
                total = term if total is None else total + term
        return total

    def far_part(k):
        all_wait(skeletons[k].at[pl.ds(0, n_blk - 1)], skel_recv.at[k])
        far = jnp.zeros((columns, rank), jnp.float32)
        for j in range(far_count):
            far = far + jnp.dot(
                skeletons[k][far_ref[0, j]], coupling_ref[j], preferred_element_type=jnp.float32
            )
        far_high = far.astype(jnp.bfloat16)
        far_low = (far - far_high.astype(jnp.float32)).astype(jnp.bfloat16)
        return jnp.concatenate([far_high, far_high, far_low], axis=1)

    def outer_part(k, l, far_all):
        far = jnp.dot(far_all, mixed[l], preferred_element_type=jnp.float32)
        return applied[l] + (near_part(k, l, False) + far)

    sublane = lax.broadcasted_iota(jnp.int32, (rank, rank), 0)
    lane = lax.broadcasted_iota(jnp.int32, (rank, rank), 1)
    as_row = jnp.broadcast_to(index_ref[...].astype(jnp.float32), (rank, rank))
    as_column = jnp.sum(jnp.where(sublane == lane, as_row, 0.0), axis=1, keepdims=True)
    point = lax.broadcasted_iota(jnp.int32, (rank, width), 1).astype(jnp.float32)
    for l in range(leaves):
        picks = jnp.where(point + float(width * l) == as_column, 1.0, 0.0).astype(jnp.bfloat16)
        mixed[l, rank : 2 * rank] = picks
        mixed[l, 2 * rank :] = picks
    firsts[0].wait()
    for l in range(leaves):
        publish(0, l, vectors[0, l])
    pl.semaphore_wait(barrier, greeted)
    send_halos(0)
    firsts[1].wait()
    send_skeleton(0)
    firsts[2].wait()
    own_load.wait()
    blank = jnp.zeros((columns, 128), jnp.float32)
    sums = {(0, 0): blank}
    curve = blank
    for l in range(leaves):
        value, total = vectors[0, l], own_part(0, l)
        applied[l] = total
        sums[0, 0] = sums[0, 0] + halves(value * value)
        curve = curve + halves(value * total)
    sum_start(SHIFT_SUM, [curve, sums[0, 0]])
    for l in range(leaves):
        loads[2 * l].wait()
        loads[2 * l + 1].wait()
        if l == leaves // 2:
            sum_next(SHIFT_SUM)
        applied[l] = applied[l] + near_part(0, l, True)
    firsts[3].wait()

    shift = None
    for k in range(APPLIES):
        far_all = far_part(k)
        for n in range(len(SHIFTS)):
            halo(k, n).wait_recv()
        if k == 0:
            line = sum_end(SHIFT_SUM)
            shift = line[:, :columns] / line[:, columns : 2 * columns]
            shift_c = per_column(shift)
        if k == APPLIES - 1:
            break
        for l in range(leaves):
            total = outer_part(k, l, far_all) - shift_c * vectors[k, l]
            vectors[k + 1, l] = total
            publish(k + 1, l, total)
        send_halos(k + 1)
        send_skeleton(k + 1)
        for j in range(k + 2):
            sums[k + 1, j] = blank
        for l in range(leaves):
            total = vectors[k + 1, l]
            for j in range(k + 2):
                sums[k + 1, j] = sums[k + 1, j] + halves(total * vectors[j, l])
        if k + 1 == APPLIES - 1:
            sum_start(GRAM_SUM, [sums[pair] for pair in PAIRS])
        for l in range(leaves):
            if k + 1 == APPLIES - 1 and l == leaves // 2:
                sum_next(GRAM_SUM)
            applied[l] = own_part(k + 1, l) + near_part(k + 1, l, True)

    line = sum_end(GRAM_SUM)
    gram = {pair: line[:, i * columns : (i + 1) * columns] for i, pair in enumerate(PAIRS)}
    x, r, p, norm = plan(gram, shift, columns)
    u = [shift * p[0], p[0] + shift * p[1], p[1] + shift * p[2], p[2]]
    x_c, r_c, p_c, u_c = ([per_column(value) for value in values] for values in (x, r, p, u))
    data = sum(x[j] * gram[j, 0] for j in range(APPLIES - 1))
    data_turn = sum(p[j] * gram[j, 0] for j in range(APPLIES))

    def combine(factors, values):
        total = factors[0] * values[0]
        for factor, value in zip(factors[1:], values[1:]):
            total = total + factor * value
        return total

    curve = blank
    for l in range(leaves):
        values = [vectors[j, l] for j in range(APPLIES)]
        x_ref[l] = combine(x_c, values)
        r_ref[l] = combine(r_c, values)
        direction = combine(p_c, values)
        p_ref[l] = direction
        total = combine(u_c, values) + p_c[-1] * outer_part(APPLIES - 1, l, far_all)
        u_ref[l] = total
        curve = curve + halves(direction * total)
    sum_start(LAST_SUM, [curve])
    sum_next(LAST_SUM)
    step = norm / sum_end(LAST_SUM)[:, :columns]
    step_c = per_column(step)
    for l in range(leaves):
        x_ref[l] = x_ref[l] + step_c * p_ref[l]
        r_ref[l] = r_ref[l] - step_c * u_ref[l]
    quadratic_ref[...] = (data + step * data_turn) * (1.0 / tracers)

    outs = [
        pltpu.make_async_copy(source, target, out_sem.at[i])
        for i, (source, target) in enumerate((
            (x_ref, solution_out), (r_ref, residual_out), (quadratic_ref, quadratic_out),
        ))
    ]
    for out in outs:
        out.start()
    for k in range(APPLIES):
        for n in range(len(SHIFTS)):
            halo(k, n).wait_send()
        all_wait(skeletons[k].at[pl.ds(0, n_blk - 1)], skel_send.at[k])
    for n in range(3):
        all_wait(row_sums[n].at[pl.ds(0, n_row - 1)], row_send.at[n])
        all_wait(blk_sums[n].at[pl.ds(0, n_blk - 1)], blk_send.at[n])
    for out in outs:
        out.wait()


def hand_over(solution_in, residual_in, quadratic_in, solution_ref, residual_ref, quadratic_ref):
    solution_ref[...] = solution_in[...]
    residual_ref[...] = residual_in[...]
    quadratic_ref[...] = quadratic_in[...]


def local(
    n_row, n_blk,
    right_side, noise_level, near_blocks, skeleton_basis, skeleton_index, far_list, couplings,
):
    leaves, columns, width = right_side.shape[2:]
    rank = skeleton_basis.shape[3]
    field = jax.ShapeDtypeStruct((leaves, columns, width), jnp.float32)
    shapes = (field, field, jax.ShapeDtypeStruct((1, columns), jnp.float32))
    vmem = pl.BlockSpec(memory_space=pltpu.VMEM)
    hbm = pl.BlockSpec(memory_space=pltpu.HBM)
    free = pl.BlockSpec(memory_space=pl.ANY)
    dma = pltpu.SemaphoreType.DMA
    outs = pl.pallas_call(
        functools.partial(kernel, n_row, n_blk, n_row * n_blk * leaves * width),
        out_shape=shapes,
        in_specs=[
            hbm, hbm, hbm, hbm, vmem, pl.BlockSpec(memory_space=pltpu.SMEM), hbm,
        ],
        out_specs=(free, free, free),
        scratch_shapes=[
            pltpu.VMEM((APPLIES, leaves, columns, width), jnp.float32),
            pltpu.VMEM(noise_level.shape[2:], jnp.float32),
            pltpu.VMEM(couplings.shape[2:], jnp.bfloat16),
            pltpu.VMEM(near_blocks.shape[2:], jnp.bfloat16),
            pltpu.VMEM((leaves, 3 * rank, width), jnp.bfloat16),
            pltpu.VMEM((APPLIES, LEAF_ROWS + 2, LEAF_COLS + 2, columns, width), jnp.bfloat16),
            pltpu.VMEM((leaves, columns, width), jnp.float32),
            pltpu.VMEM((4, leaves, columns, width), jnp.float32),
            *(pltpu.VMEM((n_blk, columns, rank), jnp.bfloat16) for _ in range(APPLIES)),
            *(pltpu.VMEM((n_row, 1, lanes), jnp.float32) for lanes in SUM_LANES),
            *(pltpu.VMEM((n_blk, 1, lanes), jnp.float32) for lanes in SUM_LANES),
            pltpu.VMEM((1, columns), jnp.float32),
            dma((4,)), dma, dma((leaves, 2)),
            dma((APPLIES, 8)), dma((APPLIES, 8)),
            dma((APPLIES,)), dma((APPLIES,)),
            dma((3,)), dma((3,)), dma((3,)), dma((3,)), dma((3,)),
        ],
        compiler_params=pltpu.CompilerParams(
            collective_id=0, has_side_effects=True, vmem_limit_bytes=64512 * 1024
        ),
    )(
        right_side[0, 0], noise_level[0, 0], near_blocks[0, 0], skeleton_basis[0, 0],
        skeleton_index[0], far_list[0], couplings[0, 0],
    )
    solution_out, residual_out, quadratic = pl.pallas_call(
        hand_over,
        out_shape=shapes,
        in_specs=[vmem, vmem, vmem],
        out_specs=(vmem, vmem, vmem),
        compiler_params=pltpu.CompilerParams(vmem_limit_bytes=4 * 1024 * 1024),
    )(*outs)
    return solution_out[None, None], residual_out[None, None], quadratic[0]


def solution(mesh):
    return jax.shard_map(
        functools.partial(local, mesh.shape["row"], mesh.shape["blk"]),
        mesh=mesh,
        in_specs=(
            P("row", "blk", None, None, None),
            P("row", "blk", None, None),
            P("row", "blk", None, None, None, None),
            P("row", "blk", None, None, None),
            P("row", "blk", None),
            P("row", "blk", None),
            P("row", "blk", None, None, None),
        ),
        out_specs=(P("row", "blk", None, None, None), P("row", "blk", None, None, None), P()),
        check_vma=False,
    )
```

```python
import functools

import jax
import jax.numpy as jnp
from jax import lax
from jax.experimental import pallas as pl
from jax.experimental.pallas import tpu as pltpu
from jax.sharding import PartitionSpec as P

LEAF_ROWS = 2
LEAF_COLS = 4
APPLIES = 4
OWN = 4
MESH = pl.DeviceIdType.MESH
SHIFTS = ((0, -1), (0, 1), (-1, -1), (-1, 1), (1, -1), (1, 1), (-1, 0), (1, 0))
SHIFT_SUM, GRAM_SUM, LAST_SUM = range(3)
SUM_LANES = (128, 384, 128)
PAIRS = tuple((i, j) for i in range(APPLIES) for j in range(i + 1))


def span(shift, count, incoming):
    if shift == 0:
        return 1, count
    if incoming:
        return (0 if shift > 0 else count + 1), 1
    return (count if shift > 0 else 1), 1


def each(count, body):
    if count <= 32:
        for i in range(count):
            body(i)
    else:
        pl.loop(0, count)(body)


def plan(gram, shift, columns):
    def inner(u, v):
        terms = {}
        for i, a in enumerate(u):
            for j, b in enumerate(v):
                key = (max(i, j), min(i, j))
                terms[key] = a * b + terms[key] if key in terms else a * b
        total = None
        for key, value in terms.items():
            term = value * gram[key]
            total = term if total is None else total + term
        return total

    def apply(u):
        out = [shift * u[0]]
        for j in range(1, len(u)):
            out.append(u[j - 1] + shift * u[j])
        return out + [u[-1]]

    one = jnp.ones((1, columns), jnp.float32)
    zero = jnp.zeros((1, columns), jnp.float32)
    x, r, p = [], [one], [one]
    norm = gram[0, 0]
    for _ in range(APPLIES - 1):
        q = apply(p)
        step = norm / inner(p, q)
        x = [a + step * b for a, b in zip(x + [zero], p)]
        r = [a - step * b for a, b in zip(r + [zero], q)]
        norm_next = inner(r, r)
        turn = norm_next / norm
        p = [a + turn * b for a, b in zip(r, p + [zero])]
        norm = norm_next
    return x, r, p, norm


def kernel(
    n_row, n_blk, tracers,
    right_hbm, noise_hbm, blocks_hbm, basis_hbm, index_ref, far_ref, coupling_hbm,
    solution_out, residual_out, quadratic_out,
    vectors, noise_ref, coupling_ref, blocks, mixed, extended, applied, ahead, skel_0, skel_1, skel_2, skel_3,
    sum_shift, sum_gram, sum_last, quadratic_ref,
    first_sem, own_sem, load_sem, halo_send, halo_recv, skel_send, skel_recv,
    sum_send, sum_recv, out_sem,
):
    leaves, columns, width = vectors.shape[1:]
    rank = basis_hbm.shape[1]
    far_count = coupling_ref.shape[0]
    my_row, my_blk = lax.axis_index("row"), lax.axis_index("blk")
    skeletons = (skel_0, skel_1, skel_2, skel_3)
    sums_all = (sum_shift, sum_gram, sum_last)
    devices = n_row * n_blk
    me = my_row * n_blk + my_blk
    parity = lax.rem(my_row, 2)
    x_ref, r_ref, p_ref, u_ref = (ahead.at[i] for i in range(4))

    firsts = [
        pltpu.make_async_copy(source, target, first_sem.at[i])
        for i, (source, target) in enumerate((
            (right_hbm, vectors.at[0]),
            (basis_hbm, mixed.at[:, pl.ds(0, rank)]),
            (noise_hbm, noise_ref),
            (coupling_hbm, coupling_ref),
        ))
    ]
    own_load = pltpu.make_async_copy(blocks_hbm.at[:, OWN], blocks.at[:, OWN], own_sem)
    loads = []
    for l in range(leaves):
        for h, part in enumerate((pl.ds(0, OWN), pl.ds(OWN + 1, 8 - OWN))):
            loads.append(pltpu.make_async_copy(blocks_hbm.at[l, part], blocks.at[l, part], load_sem.at[l, h]))
    firsts[0].start()
    firsts[1].start()
    firsts[2].start()
    own_load.start()
    firsts[3].start()
    for load in loads:
        load.start()

    def row_at(o):
        return lax.rem(my_row + (o + n_row), n_row)

    def blk_at(o):
        return lax.rem(my_blk + (o + n_blk), n_blk)

    barrier = pltpu.get_barrier_semaphore()

    def greet(row, blk):
        pl.semaphore_signal(barrier, inc=1, device_id={"row": row, "blk": blk}, device_id_type=MESH)

    each(devices - 1, lambda i: greet(row_at((i + 1) // n_blk), blk_at((i + 1) % n_blk)))

    def halo(k, n):
        dr, dc = SHIFTS[n]
        (sr, nr), (sc, nc) = span(dr, LEAF_ROWS, False), span(dc, LEAF_COLS, False)
        (tr, _), (tc, _) = span(dr, LEAF_ROWS, True), span(dc, LEAF_COLS, True)
        return pltpu.make_async_remote_copy(
            src_ref=extended.at[k, pl.ds(sr, nr), pl.ds(sc, nc)],
            dst_ref=extended.at[k, pl.ds(tr, nr), pl.ds(tc, nc)],
            send_sem=halo_send.at[k, n],
            recv_sem=halo_recv.at[k, n],
            device_id={"row": row_at(dr), "blk": blk_at(dc)},
            device_id_type=MESH,
        )

    def sum_copy(n, i):
        return pltpu.make_async_remote_copy(
            src_ref=sums_all[n].at[me],
            dst_ref=sums_all[n].at[me],
            send_sem=sum_send.at[n],
            recv_sem=sum_recv.at[n],
            device_id={"row": row_at(i // n_blk), "blk": blk_at(i % n_blk)},
            device_id_type=MESH,
        )

    def skeleton_copy(k, i):
        return pltpu.make_async_remote_copy(
            src_ref=skeletons[k].at[my_blk],
            dst_ref=skeletons[k].at[my_blk],
            send_sem=skel_send.at[k],
            recv_sem=skel_recv.at[k],
            device_id={"row": my_row, "blk": blk_at(i + 1)},
            device_id_type=MESH,
        )

    def all_wait(every, sem):
        pltpu.make_async_copy(every, every, sem).wait()

    def sum_start(n, sums):
        stacked = jnp.concatenate(sums, axis=0)
        rest = SUM_LANES[n] - stacked.shape[0]
        if rest:
            stacked = jnp.concatenate([stacked, jnp.zeros((rest, 128), jnp.float32)], axis=0)
        high = stacked.astype(jnp.bfloat16)
        left = stacked - high.astype(jnp.float32)
        middle = left.astype(jnp.bfloat16)
        low = (left - middle.astype(jnp.float32)).astype(jnp.bfloat16)
        lines = lax.dot_general(
            jnp.ones((8, 3 * 128), jnp.bfloat16), jnp.concatenate([high, middle, low], axis=1),
            (((1,), (1,)), ((), ())), preferred_element_type=jnp.float32,
        )
        sums_all[n][me] = lines[:1]
        each(devices - 1, lambda i: sum_copy(n, devices - 1 - i).start())

    def sum_end(n):
        all_wait(sums_all[n].at[pl.ds(0, devices - 1)], sum_recv.at[n])
        return jnp.sum(sums_all[n][...], axis=0)

    spread_row = lax.broadcasted_iota(jnp.int32, (columns, columns), 0)
    spread_lane = lax.broadcasted_iota(jnp.int32, (columns, columns), 1)

    def per_column(line):
        wide = jnp.broadcast_to(line, (columns, columns))
        kept = jnp.where(spread_row == spread_lane, wide, 0.0)
        return jnp.sum(kept, axis=1, keepdims=True)

    def halves(product):
        total = product[:, :128]
        for h in range(1, width // 128):
            total = total + product[:, 128 * h : 128 * (h + 1)]
        return total

    def at(l):
        a, c = divmod(l, LEAF_COLS)
        return a + 1, c + 1

    def slots(l):
        a, c = divmod(l, LEAF_COLS)
        for s in range(9):
            if s != OWN:
                yield s, a + s // 3, c + s % 3

    def inside(row, col):
        return 1 <= row <= LEAF_ROWS and 1 <= col <= LEAF_COLS

    def publish(k, l, value):
        row, col = at(l)
        extended[k, row, col] = value.astype(jnp.bfloat16)

    def send_halos(k, dc):
        for n, (_, toward) in enumerate(SHIFTS):
            if toward == dc:
                halo(k, n).start()

    def skeleton_part(k, l):
        return lax.dot_general(
            extended[(k, *at(l))], mixed[l, : 2 * rank], (((1,), (1,)), ((), ())),
            preferred_element_type=jnp.float32,
        )

    def send_skeleton(k, both):
        skeletons[k][my_blk] = (both[:, :rank] + both[:, rank:]).astype(jnp.bfloat16)
        each(n_blk - 1, lambda i: skeleton_copy(k, i).start())

    def own_part(k, l):
        value = vectors[k, l]
        high = extended[(k, *at(l))]
        low = (value - high.astype(jnp.float32)).astype(jnp.bfloat16)
        product = jnp.dot(high, blocks[l, OWN], preferred_element_type=jnp.float32)
        product = product + jnp.dot(low, blocks[l, OWN], preferred_element_type=jnp.float32)
        return noise_ref[l : l + 1] * value + product

    def near_sum(k, l, sources):
        total = None
        for s, row, col in sources:
            term = jnp.dot(extended[k, row, col], blocks[l, s], preferred_element_type=jnp.float32)
            total = term if total is None else total + term
        return total

    def inner_part(k, l):
        return near_sum(k, l, [slot for slot in slots(l) if inside(*slot[1:])])

    def row_part(k, side):
        row = (LEAF_ROWS + 1) * side
        all_wait(extended.at[k, pl.ds(row, 1), pl.ds(1, LEAF_COLS)], halo_recv.at[k, len(SHIFTS) - 1 - side])
        for c in range(LEAF_COLS):
            l = (LEAF_ROWS - 1) * LEAF_COLS * side + c
            sources = [(6 * side + g, row, c + g) for g in range(3) if 1 <= c + g <= LEAF_COLS]
            applied[l] = applied[l] + near_sum(k, l, sources)

    def column_part(k, side):
        for n, (_, toward) in enumerate(SHIFTS):
            if toward == (-1 if side else 1):
                halo(k, n).wait_recv()
        for l in range(leaves):
            edge = (LEAF_COLS + 1) * side
            sources = [slot for slot in slots(l) if slot[2] == edge]
            if sources:
                applied[l] = applied[l] + near_sum(k, l, sources)

    def far_part(k):
        all_wait(skeletons[k].at[pl.ds(0, n_blk - 1)], skel_recv.at[k])
        far = jnp.zeros((columns, rank), jnp.float32)
        for j in range(far_count):
            far = far + jnp.dot(
                skeletons[k][far_ref[0, j]], coupling_ref[j], preferred_element_type=jnp.float32
            )
        far_high = far.astype(jnp.bfloat16)
        far_low = (far - far_high.astype(jnp.float32)).astype(jnp.bfloat16)
        return jnp.concatenate([far_high, far_high, far_low], axis=1)

    def outer_parts(k):
        row_part(k, 1 - parity)
        row_part(k, parity)
        column_part(k, 0)
        column_part(k, 1)
        return far_part(k)

    def whole(k, l, far_all):
        return applied[l] + jnp.dot(far_all, mixed[l], preferred_element_type=jnp.float32)

    left_edge = [l for l in range(leaves) if l % LEAF_COLS == 0]
    right_edge = [l for l in range(leaves) if l % LEAF_COLS == LEAF_COLS - 1]
    middle = [l for l in range(leaves) if l not in left_edge + right_edge]
    stages = ((left_edge, -1), (right_edge, 1), (middle, 0))

    sublane = lax.broadcasted_iota(jnp.int32, (rank, rank), 0)
    lane = lax.broadcasted_iota(jnp.int32, (rank, rank), 1)
    as_row = jnp.broadcast_to(index_ref[...].astype(jnp.float32), (rank, rank))
    as_column = jnp.sum(jnp.where(sublane == lane, as_row, 0.0), axis=1, keepdims=True)
    point = lax.broadcasted_iota(jnp.int32, (rank, width), 1).astype(jnp.float32)
    for l in range(leaves):
        picks = jnp.where(point + float(width * l) == as_column, 1.0, 0.0).astype(jnp.bfloat16)
        mixed[l, rank : 2 * rank] = picks
        mixed[l, 2 * rank :] = picks
    firsts[0].wait()
    for l in range(leaves):
        publish(0, l, vectors[0, l])
    pl.semaphore_wait(barrier, devices - 1)
    for dc in (-1, 1, 0):
        send_halos(0, dc)
    firsts[1].wait()
    send_skeleton(0, sum(skeleton_part(0, l) for l in range(leaves)))
    firsts[2].wait()
    own_load.wait()
    blank = jnp.zeros((columns, 128), jnp.float32)
    sums = {(0, 0): blank}
    curve = blank
    for l in range(leaves):
        value, total = vectors[0, l], own_part(0, l)
        applied[l] = total
        sums[0, 0] = sums[0, 0] + halves(value * value)
        curve = curve + halves(value * total)
    sum_start(SHIFT_SUM, [curve, sums[0, 0]])
    for l in range(leaves):
        loads[2 * l].wait()
        loads[2 * l + 1].wait()
        applied[l] = applied[l] + inner_part(0, l)
    firsts[3].wait()

    shift = None
    for k in range(APPLIES):
        far_all = outer_parts(k)
        if k == 0:
            line = sum_end(SHIFT_SUM)
            shift = line[:, :columns] / line[:, columns : 2 * columns]
            shift_c = per_column(shift)
        if k == APPLIES - 1:
            break
        both = jnp.zeros((columns, 2 * rank), jnp.float32)
        for some, dc in stages:
            for l in some:
                total = whole(k, l, far_all) - shift_c * vectors[k, l]
                vectors[k + 1, l] = total
                publish(k + 1, l, total)
                both = both + skeleton_part(k + 1, l)
            send_halos(k + 1, dc)
        send_skeleton(k + 1, both)
        for j in range(k + 2):
            sums[k + 1, j] = blank
        for l in range(leaves):
            total = vectors[k + 1, l]
            for j in range(k + 2):
                sums[k + 1, j] = sums[k + 1, j] + halves(total * vectors[j, l])
        if k + 1 == APPLIES - 1:
            sum_start(GRAM_SUM, [sums[pair] for pair in PAIRS])
        for l in range(leaves):
            applied[l] = own_part(k + 1, l) + inner_part(k + 1, l)

    line = sum_end(GRAM_SUM)
    gram = {pair: line[:, i * columns : (i + 1) * columns] for i, pair in enumerate(PAIRS)}
    x, r, p, norm = plan(gram, shift, columns)
    u = [shift * p[0], p[0] + shift * p[1], p[1] + shift * p[2], p[2]]
    x_c, r_c, p_c, u_c = ([per_column(value) for value in values] for values in (x, r, p, u))
    data = sum(x[j] * gram[j, 0] for j in range(APPLIES - 1))
    data_turn = sum(p[j] * gram[j, 0] for j in range(APPLIES))

    def combine(factors, values):
        total = factors[0] * values[0]
        for factor, value in zip(factors[1:], values[1:]):
            total = total + factor * value
        return total

    curve = blank
    for l in range(leaves):
        values = [vectors[j, l] for j in range(APPLIES)]
        x_ref[l] = combine(x_c, values)
        r_ref[l] = combine(r_c, values)
        direction = combine(p_c, values)
        p_ref[l] = direction
        total = combine(u_c, values) + p_c[-1] * whole(APPLIES - 1, l, far_all)
        u_ref[l] = total
        curve = curve + halves(direction * total)
    sum_start(LAST_SUM, [curve])
    step = norm / sum_end(LAST_SUM)[:, :columns]
    step_c = per_column(step)
    for l in range(leaves):
        x_ref[l] = x_ref[l] + step_c * p_ref[l]
        r_ref[l] = r_ref[l] - step_c * u_ref[l]
    quadratic_ref[...] = (data + step * data_turn) * (1.0 / tracers)

    outs = [
        pltpu.make_async_copy(source, target, out_sem.at[i])
        for i, (source, target) in enumerate((
            (x_ref, solution_out), (r_ref, residual_out), (quadratic_ref, quadratic_out),
        ))
    ]
    for out in outs:
        out.start()
    for k in range(APPLIES):
        for n in range(len(SHIFTS)):
            halo(k, n).wait_send()
        all_wait(skeletons[k].at[pl.ds(0, n_blk - 1)], skel_send.at[k])
    for n in range(3):
        all_wait(sums_all[n].at[pl.ds(0, devices - 1)], sum_send.at[n])
    for out in outs:
        out.wait()


def hand_over(
    solution_in, residual_in, quadratic_in, solution_out, residual_out, quadratic_out,
    solution_held, residual_held, quadratic_held, in_sem, out_sem,
):
    held = (solution_held, residual_held, quadratic_held)
    ins = [
        pltpu.make_async_copy(source, slot, in_sem.at[i])
        for i, (source, slot) in enumerate(zip((solution_in, residual_in, quadratic_in), held))
    ]
    outs = [
        pltpu.make_async_copy(slot, target, out_sem.at[i])
        for i, (slot, target) in enumerate(zip(held, (solution_out, residual_out, quadratic_out)))
    ]
    for copy in ins:
        copy.start()
    for copy, out in zip(ins, outs):
        copy.wait()
        out.start()
    for out in outs:
        out.wait()


def local(
    n_row, n_blk,
    right_side, noise_level, near_blocks, skeleton_basis, skeleton_index, far_list, couplings,
):
    leaves, columns, width = right_side.shape[2:]
    rank = skeleton_basis.shape[3]
    field = jax.ShapeDtypeStruct((leaves, columns, width), jnp.float32)
    shapes = (field, field, jax.ShapeDtypeStruct((1, columns), jnp.float32))
    vmem = pl.BlockSpec(memory_space=pltpu.VMEM)
    hbm = pl.BlockSpec(memory_space=pltpu.HBM)
    free = pl.BlockSpec(memory_space=pl.ANY)
    dma = pltpu.SemaphoreType.DMA
    outs = pl.pallas_call(
        functools.partial(kernel, n_row, n_blk, n_row * n_blk * leaves * width),
        out_shape=shapes,
        in_specs=[
            hbm, hbm, hbm, hbm, vmem, pl.BlockSpec(memory_space=pltpu.SMEM), hbm,
        ],
        out_specs=(free, free, free),
        scratch_shapes=[
            pltpu.VMEM((APPLIES, leaves, columns, width), jnp.float32),
            pltpu.VMEM(noise_level.shape[2:], jnp.float32),
            pltpu.VMEM(couplings.shape[2:], jnp.bfloat16),
            pltpu.VMEM(near_blocks.shape[2:], jnp.bfloat16),
            pltpu.VMEM((leaves, 3 * rank, width), jnp.bfloat16),
            pltpu.VMEM((APPLIES, LEAF_ROWS + 2, LEAF_COLS + 2, columns, width), jnp.bfloat16),
            pltpu.VMEM((leaves, columns, width), jnp.float32),
            pltpu.VMEM((4, leaves, columns, width), jnp.float32),
            *(pltpu.VMEM((n_blk, columns, rank), jnp.bfloat16) for _ in range(APPLIES)),
            *(pltpu.VMEM((n_row * n_blk, 1, lanes), jnp.float32) for lanes in SUM_LANES),
            pltpu.VMEM((1, columns), jnp.float32),
            dma((4,)), dma, dma((leaves, 2)),
            dma((APPLIES, 8)), dma((APPLIES, 8)),
            dma((APPLIES,)), dma((APPLIES,)),
            dma((3,)), dma((3,)), dma((3,)),
        ],
        compiler_params=pltpu.CompilerParams(
            collective_id=0, has_side_effects=True, vmem_limit_bytes=64512 * 1024
        ),
    )(
        right_side[0, 0], noise_level[0, 0], near_blocks[0, 0], skeleton_basis[0, 0],
        skeleton_index[0], far_list[0], couplings[0, 0],
    )
    solution_out, residual_out, quadratic = pl.pallas_call(
        hand_over,
        out_shape=shapes,
        in_specs=[free, free, free],
        out_specs=(free, free, free),
        scratch_shapes=[*(pltpu.VMEM(shape.shape, shape.dtype) for shape in shapes), dma((3,)), dma((3,))],
        compiler_params=pltpu.CompilerParams(vmem_limit_bytes=63 * 1024 * 1024),
    )(*outs)
    return solution_out[None, None], residual_out[None, None], quadratic[0]


def solution(mesh):
    return jax.shard_map(
        functools.partial(local, mesh.shape["row"], mesh.shape["blk"]),
        mesh=mesh,
        in_specs=(
            P("row", "blk", None, None, None),
            P("row", "blk", None, None),
            P("row", "blk", None, None, None, None),
            P("row", "blk", None, None, None),
            P("row", "blk", None),
            P("row", "blk", None),
            P("row", "blk", None, None, None),
        ),
        out_specs=(P("row", "blk", None, None, None), P("row", "blk", None, None, None), P()),
        check_vma=False,
    )
```

```python
import functools

import jax
import jax.numpy as jnp
from jax import lax
from jax.experimental import pallas as pl
from jax.experimental.pallas import tpu as pltpu
from jax.sharding import PartitionSpec as P

LEAF_ROWS = 2
LEAF_COLS = 4
APPLIES = 4
OWN = 4
MESH = pl.DeviceIdType.MESH
SHIFTS = ((0, -1), (0, 1), (-1, -1), (-1, 1), (1, -1), (1, 1), (-1, 0), (1, 0))
SHIFT_SUM, GRAM_SUM, LAST_SUM = range(3)
SUM_LANES = (128, 384, 128)
PAIRS = tuple((i, j) for i in range(APPLIES) for j in range(i + 1))


def span(shift, count, incoming):
    if shift == 0:
        return 1, count
    if incoming:
        return (0 if shift > 0 else count + 1), 1
    return (count if shift > 0 else 1), 1


def each(count, body):
    if count <= 32:
        for i in range(count):
            body(i)
    else:
        pl.loop(0, count)(body)


def plan(gram, shift, columns):
    def inner(u, v):
        terms = {}
        for i, a in enumerate(u):
            for j, b in enumerate(v):
                key = (max(i, j), min(i, j))
                terms[key] = a * b + terms[key] if key in terms else a * b
        total = None
        for key, value in terms.items():
            term = value * gram[key]
            total = term if total is None else total + term
        return total

    def apply(u):
        out = [shift * u[0]]
        for j in range(1, len(u)):
            out.append(u[j - 1] + shift * u[j])
        return out + [u[-1]]

    one = jnp.ones((1, columns), jnp.float32)
    zero = jnp.zeros((1, columns), jnp.float32)
    x, r, p = [], [one], [one]
    norm = gram[0, 0]
    for _ in range(APPLIES - 1):
        q = apply(p)
        step = norm / inner(p, q)
        x = [a + step * b for a, b in zip(x + [zero], p)]
        r = [a - step * b for a, b in zip(r + [zero], q)]
        norm_next = inner(r, r)
        turn = norm_next / norm
        p = [a + turn * b for a, b in zip(r, p + [zero])]
        norm = norm_next
    return x, r, p, norm


def kernel(
    n_row, n_blk, tracers,
    right_hbm, noise_hbm, blocks_hbm, basis_hbm, index_ref, far_ref, coupling_hbm,
    solution_out, residual_out, quadratic_out,
    vectors, noise_ref, coupling_ref, coupling_twice, blocks, mixed, extended, applied, ahead, skel_0, skel_1, skel_2, skel_3,
    sum_shift, sum_gram, sum_last, quadratic_ref,
    first_sem, own_sem, load_sem, halo_send, halo_recv, skel_send, skel_recv,
    sum_send, sum_recv, out_sem,
):
    leaves, columns, width = vectors.shape[1:]
    rank = basis_hbm.shape[1]
    far_count = coupling_ref.shape[0]
    my_row, my_blk = lax.axis_index("row"), lax.axis_index("blk")
    skeletons = (skel_0, skel_1, skel_2, skel_3)
    sums_all = (sum_shift, sum_gram, sum_last)
    devices = n_row * n_blk
    me = my_row * n_blk + my_blk
    parity = lax.rem(my_row, 2)
    x_ref, r_ref, p_ref, u_ref = (ahead.at[i] for i in range(4))

    firsts = [
        pltpu.make_async_copy(source, target, first_sem.at[i])
        for i, (source, target) in enumerate((
            (right_hbm, vectors.at[0]),
            (basis_hbm, mixed.at[:, pl.ds(0, rank)]),
            (noise_hbm, noise_ref),
            (coupling_hbm, coupling_ref),
        ))
    ]
    own_load = pltpu.make_async_copy(blocks_hbm.at[:, OWN], blocks.at[:, OWN], own_sem)
    loads = []
    for l in range(leaves):
        for h, part in enumerate((pl.ds(0, OWN), pl.ds(OWN + 1, 8 - OWN))):
            loads.append(pltpu.make_async_copy(blocks_hbm.at[l, part], blocks.at[l, part], load_sem.at[l, h]))
    firsts[0].start()
    firsts[1].start()
    firsts[2].start()
    own_load.start()
    firsts[3].start()
    for load in loads:
        load.start()

    def row_at(o):
        return lax.rem(my_row + (o + n_row), n_row)

    def blk_at(o):
        return lax.rem(my_blk + (o + n_blk), n_blk)

    barrier = pltpu.get_barrier_semaphore()

    def greet(row, blk):
        pl.semaphore_signal(barrier, inc=1, device_id={"row": row, "blk": blk}, device_id_type=MESH)

    each(devices - 1, lambda i: greet(row_at((i + 1) // n_blk), blk_at((i + 1) % n_blk)))

    def halo(k, n):
        dr, dc = SHIFTS[n]
        (sr, nr), (sc, nc) = span(dr, LEAF_ROWS, False), span(dc, LEAF_COLS, False)
        (tr, _), (tc, _) = span(dr, LEAF_ROWS, True), span(dc, LEAF_COLS, True)
        return pltpu.make_async_remote_copy(
            src_ref=extended.at[k, pl.ds(sr, nr), pl.ds(sc, nc)],
            dst_ref=extended.at[k, pl.ds(tr, nr), pl.ds(tc, nc)],
            send_sem=halo_send.at[k, n],
            recv_sem=halo_recv.at[k, n],
            device_id={"row": row_at(dr), "blk": blk_at(dc)},
            device_id_type=MESH,
        )

    def sum_copy(n, i):
        return pltpu.make_async_remote_copy(
            src_ref=sums_all[n].at[me],
            dst_ref=sums_all[n].at[me],
            send_sem=sum_send.at[n],
            recv_sem=sum_recv.at[n],
            device_id={"row": row_at(i // n_blk), "blk": blk_at(i % n_blk)},
            device_id_type=MESH,
        )

    def skeleton_copy(k, i):
        return pltpu.make_async_remote_copy(
            src_ref=skeletons[k].at[my_blk],
            dst_ref=skeletons[k].at[my_blk],
            send_sem=skel_send.at[k],
            recv_sem=skel_recv.at[k],
            device_id={"row": my_row, "blk": blk_at(i + 1)},
            device_id_type=MESH,
        )

    def all_wait(every, sem):
        pltpu.make_async_copy(every, every, sem).wait()

    def sum_start(n, sums):
        stacked = jnp.concatenate(sums, axis=0)
        rest = SUM_LANES[n] - stacked.shape[0]
        if rest:
            stacked = jnp.concatenate([stacked, jnp.zeros((rest, 128), jnp.float32)], axis=0)
        high = stacked.astype(jnp.bfloat16)
        left = stacked - high.astype(jnp.float32)
        middle = left.astype(jnp.bfloat16)
        low = (left - middle.astype(jnp.float32)).astype(jnp.bfloat16)
        lines = lax.dot_general(
            jnp.ones((8, 3 * 128), jnp.bfloat16), jnp.concatenate([high, middle, low], axis=1),
            (((1,), (1,)), ((), ())), preferred_element_type=jnp.float32,
        )
        sums_all[n][me] = lines[:1]
        each(devices - 1, lambda i: sum_copy(n, devices - 1 - i).start())

    def sum_end(n):
        all_wait(sums_all[n].at[pl.ds(0, devices - 1)], sum_recv.at[n])
        return jnp.sum(sums_all[n][...], axis=0)

    spread_row = lax.broadcasted_iota(jnp.int32, (columns, columns), 0)
    spread_lane = lax.broadcasted_iota(jnp.int32, (columns, columns), 1)

    def per_column(line):
        wide = jnp.broadcast_to(line, (columns, columns))
        kept = jnp.where(spread_row == spread_lane, wide, 0.0)
        return jnp.sum(kept, axis=1, keepdims=True)

    def halves(product):
        total = product[:, :128]
        for h in range(1, width // 128):
            total = total + product[:, 128 * h : 128 * (h + 1)]
        return total

    def at(l):
        a, c = divmod(l, LEAF_COLS)
        return a + 1, c + 1

    def slots(l):
        a, c = divmod(l, LEAF_COLS)
        for s in range(9):
            if s != OWN:
                yield s, a + s // 3, c + s % 3

    def inside(row, col):
        return 1 <= row <= LEAF_ROWS and 1 <= col <= LEAF_COLS

    def publish(k, l, value):
        row, col = at(l)
        extended[k, row, col] = value.astype(jnp.bfloat16)

    def send_halos(k, dc):
        for n, (_, toward) in enumerate(SHIFTS):
            if toward == dc:
                halo(k, n).start()

    def skeleton_part(k, l):
        return lax.dot_general(
            extended[(k, *at(l))], mixed[l], (((1,), (1,)), ((), ())),
            preferred_element_type=jnp.float32,
        )

    def send_skeleton(k, both):
        skeletons[k][my_blk] = (both[:, :rank] + both[:, rank:]).astype(jnp.bfloat16)
        each(n_blk - 1, lambda i: skeleton_copy(k, i).start())

    def own_part(k, l):
        value = vectors[k, l]
        high = extended[(k, *at(l))]
        low = (value - high.astype(jnp.float32)).astype(jnp.bfloat16)
        product = jnp.dot(high, blocks[l, OWN], preferred_element_type=jnp.float32)
        product = product + jnp.dot(low, blocks[l, OWN], preferred_element_type=jnp.float32)
        return noise_ref[l : l + 1] * value + product

    def near_sum(k, l, sources):
        total = None
        for s, row, col in sources:
            term = jnp.dot(extended[k, row, col], blocks[l, s], preferred_element_type=jnp.float32)
            total = term if total is None else total + term
        return total

    def inner_part(k, l):
        return near_sum(k, l, [slot for slot in slots(l) if inside(*slot[1:])])

    def row_part(k, side):
        row = (LEAF_ROWS + 1) * side
        all_wait(extended.at[k, pl.ds(row, 1), pl.ds(1, LEAF_COLS)], halo_recv.at[k, len(SHIFTS) - 1 - side])
        for c in range(LEAF_COLS):
            l = (LEAF_ROWS - 1) * LEAF_COLS * side + c
            sources = [(6 * side + g, row, c + g) for g in range(3) if 1 <= c + g <= LEAF_COLS]
            applied[l] = applied[l] + near_sum(k, l, sources)

    def column_part(k, side):
        for n, (_, toward) in enumerate(SHIFTS):
            if toward == (-1 if side else 1):
                halo(k, n).wait_recv()
        for l in range(leaves):
            edge = (LEAF_COLS + 1) * side
            sources = [slot for slot in slots(l) if slot[2] == edge]
            if sources:
                applied[l] = applied[l] + near_sum(k, l, sources)

    def far_part(k):
        all_wait(skeletons[k].at[pl.ds(0, n_blk - 1)], skel_recv.at[k])
        far = jnp.zeros((columns, 2 * rank), jnp.float32)
        for j in range(far_count):
            far = far + jnp.dot(
                skeletons[k][far_ref[0, j]], coupling_twice[j], preferred_element_type=jnp.float32
            )
        return far.astype(jnp.bfloat16)

    def outer_parts(k):
        row_part(k, 1 - parity)
        row_part(k, parity)
        column_part(k, 0)
        column_part(k, 1)
        far_all = far_part(k)
        if k == APPLIES - 1:
            ahead_values.extend(look_ahead())
        return far_all

    def whole(k, l, far_all):
        return applied[l] + jnp.dot(far_all, mixed[l], preferred_element_type=jnp.float32)

    left_edge = [l for l in range(leaves) if l % LEAF_COLS == 0]
    right_edge = [l for l in range(leaves) if l % LEAF_COLS == LEAF_COLS - 1]
    middle = [l for l in range(leaves) if l not in left_edge + right_edge]
    stages = ((left_edge, -1), (right_edge, 1), (middle, 0))

    sublane = lax.broadcasted_iota(jnp.int32, (rank, rank), 0)
    lane = lax.broadcasted_iota(jnp.int32, (rank, rank), 1)
    as_row = jnp.broadcast_to(index_ref[...].astype(jnp.float32), (rank, rank))
    as_column = jnp.sum(jnp.where(sublane == lane, as_row, 0.0), axis=1, keepdims=True)
    point = lax.broadcasted_iota(jnp.int32, (rank, width), 1).astype(jnp.float32)
    for l in range(leaves):
        picks = jnp.where(point + float(width * l) == as_column, 1.0, 0.0).astype(jnp.bfloat16)
        mixed[l, rank:] = picks
    firsts[0].wait()
    for l in range(leaves):
        publish(0, l, vectors[0, l])
    pl.semaphore_wait(barrier, devices - 1)
    for dc in (-1, 1, 0):
        send_halos(0, dc)
    firsts[1].wait()
    send_skeleton(0, sum(skeleton_part(0, l) for l in range(leaves)))
    firsts[2].wait()
    own_load.wait()
    blank = jnp.zeros((columns, 128), jnp.float32)
    sums = {(0, 0): blank}
    curve = blank
    for l in range(leaves):
        value, total = vectors[0, l], own_part(0, l)
        applied[l] = total
        sums[0, 0] = sums[0, 0] + halves(value * value)
        curve = curve + halves(value * total)
    sum_start(SHIFT_SUM, [curve, sums[0, 0]])
    for l in range(leaves):
        loads[2 * l].wait()
        loads[2 * l + 1].wait()
        applied[l] = applied[l] + inner_part(0, l)
    firsts[3].wait()
    for j in range(far_count):
        coupling = coupling_ref[j]
        coupling_twice[j] = jnp.concatenate([coupling, coupling], axis=1)

    def combine(factors, values):
        total = factors[0] * values[0]
        for factor, value in zip(factors[1:], values[1:]):
            total = total + factor * value
        return total

    def look_ahead():
        line = sum_end(GRAM_SUM)
        gram = {pair: line[:, i * columns : (i + 1) * columns] for i, pair in enumerate(PAIRS)}
        x, r, p, norm = plan(gram, shift, columns)
        u = [shift * p[0], p[0] + shift * p[1], p[1] + shift * p[2], p[2]]
        x_c, r_c, p_c, u_c = ([per_column(value) for value in values] for values in (x, r, p, u))
        data = sum(x[j] * gram[j, 0] for j in range(APPLIES - 1))
        data_turn = sum(p[j] * gram[j, 0] for j in range(APPLIES))
        for l in range(leaves):
            values = [vectors[j, l] for j in range(APPLIES)]
            x_ref[l] = combine(x_c, values)
            r_ref[l] = combine(r_c, values)
            p_ref[l] = combine(p_c, values)
            u_ref[l] = combine(u_c, values)
        return norm, data, data_turn, p_c[-1]

    shift, ahead_values = None, []
    for k in range(APPLIES):
        far_all = outer_parts(k)
        if k == 0:
            line = sum_end(SHIFT_SUM)
            shift = line[:, :columns] / line[:, columns : 2 * columns]
            shift_c = per_column(shift)
        if k == APPLIES - 1:
            break
        both = jnp.zeros((columns, 2 * rank), jnp.float32)
        for some, dc in stages:
            for l in some:
                total = whole(k, l, far_all) - shift_c * vectors[k, l]
                vectors[k + 1, l] = total
                publish(k + 1, l, total)
                both = both + skeleton_part(k + 1, l)
            if not dc:
                send_skeleton(k + 1, both)
            send_halos(k + 1, dc)
        for j in range(k + 2):
            sums[k + 1, j] = blank
        for l in range(leaves):
            total = vectors[k + 1, l]
            for j in range(k + 2):
                sums[k + 1, j] = sums[k + 1, j] + halves(total * vectors[j, l])
        if k + 1 == APPLIES - 1:
            sum_start(GRAM_SUM, [sums[pair] for pair in PAIRS])
        for l in range(leaves):
            applied[l] = own_part(k + 1, l) + inner_part(k + 1, l)

    norm, data, data_turn, p_last = ahead_values
    curve = blank
    for l in range(leaves):
        total = u_ref[l] + p_last * whole(APPLIES - 1, l, far_all)
        u_ref[l] = total
        curve = curve + halves(p_ref[l] * total)
    sum_start(LAST_SUM, [curve])
    step = norm / sum_end(LAST_SUM)[:, :columns]
    step_c = per_column(step)
    for l in range(leaves):
        x_ref[l] = x_ref[l] + step_c * p_ref[l]
        r_ref[l] = r_ref[l] - step_c * u_ref[l]
    quadratic_ref[...] = (data + step * data_turn) * (1.0 / tracers)

    outs = [
        pltpu.make_async_copy(source, target, out_sem.at[i])
        for i, (source, target) in enumerate((
            (x_ref, solution_out), (r_ref, residual_out), (quadratic_ref, quadratic_out),
        ))
    ]
    for out in outs:
        out.start()
    for k in range(APPLIES):
        for n in range(len(SHIFTS)):
            halo(k, n).wait_send()
        all_wait(skeletons[k].at[pl.ds(0, n_blk - 1)], skel_send.at[k])
    for n in range(3):
        all_wait(sums_all[n].at[pl.ds(0, devices - 1)], sum_send.at[n])
    for out in outs:
        out.wait()


def hand_over(
    solution_in, residual_in, quadratic_in, solution_out, residual_out, quadratic_out,
    solution_held, residual_held, quadratic_held, in_sem, out_sem,
):
    held = (solution_held, residual_held, quadratic_held)
    ins = [
        pltpu.make_async_copy(source, slot, in_sem.at[i])
        for i, (source, slot) in enumerate(zip((solution_in, residual_in, quadratic_in), held))
    ]
    outs = [
        pltpu.make_async_copy(slot, target, out_sem.at[i])
        for i, (slot, target) in enumerate(zip(held, (solution_out, residual_out, quadratic_out)))
    ]
    for copy in ins:
        copy.start()
    for copy, out in zip(ins, outs):
        copy.wait()
        out.start()
    for out in outs:
        out.wait()


def local(
    n_row, n_blk,
    right_side, noise_level, near_blocks, skeleton_basis, skeleton_index, far_list, couplings,
):
    leaves, columns, width = right_side.shape[2:]
    rank = skeleton_basis.shape[3]
    field = jax.ShapeDtypeStruct((leaves, columns, width), jnp.float32)
    shapes = (field, field, jax.ShapeDtypeStruct((1, columns), jnp.float32))
    vmem = pl.BlockSpec(memory_space=pltpu.VMEM)
    hbm = pl.BlockSpec(memory_space=pltpu.HBM)
    free = pl.BlockSpec(memory_space=pl.ANY)
    dma = pltpu.SemaphoreType.DMA
    outs = pl.pallas_call(
        functools.partial(kernel, n_row, n_blk, n_row * n_blk * leaves * width),
        out_shape=shapes,
        in_specs=[
            hbm, hbm, hbm, hbm, vmem, pl.BlockSpec(memory_space=pltpu.SMEM), hbm,
        ],
        out_specs=(free, free, free),
        scratch_shapes=[
            pltpu.VMEM((APPLIES, leaves, columns, width), jnp.float32),
            pltpu.VMEM(noise_level.shape[2:], jnp.float32),
            pltpu.VMEM(couplings.shape[2:], jnp.bfloat16),
            pltpu.VMEM((couplings.shape[2], rank, 2 * rank), jnp.bfloat16),
            pltpu.VMEM(near_blocks.shape[2:], jnp.bfloat16),
            pltpu.VMEM((leaves, 2 * rank, width), jnp.bfloat16),
            pltpu.VMEM((APPLIES, LEAF_ROWS + 2, LEAF_COLS + 2, columns, width), jnp.bfloat16),
            pltpu.VMEM((leaves, columns, width), jnp.float32),
            pltpu.VMEM((4, leaves, columns, width), jnp.float32),
            *(pltpu.VMEM((n_blk, columns, rank), jnp.bfloat16) for _ in range(APPLIES)),
            *(pltpu.VMEM((n_row * n_blk, 1, lanes), jnp.float32) for lanes in SUM_LANES),
            pltpu.VMEM((1, columns), jnp.float32),
            dma((4,)), dma, dma((leaves, 2)),
            dma((APPLIES, 8)), dma((APPLIES, 8)),
            dma((APPLIES,)), dma((APPLIES,)),
            dma((3,)), dma((3,)), dma((3,)),
        ],
        compiler_params=pltpu.CompilerParams(
            collective_id=0, has_side_effects=True, vmem_limit_bytes=64512 * 1024
        ),
    )(
        right_side[0, 0], noise_level[0, 0], near_blocks[0, 0], skeleton_basis[0, 0],
        skeleton_index[0], far_list[0], couplings[0, 0],
    )
    solution_out, residual_out, quadratic = pl.pallas_call(
        hand_over,
        out_shape=shapes,
        in_specs=[free, free, free],
        out_specs=(free, free, free),
        scratch_shapes=[*(pltpu.VMEM(shape.shape, shape.dtype) for shape in shapes), dma((3,)), dma((3,))],
        compiler_params=pltpu.CompilerParams(vmem_limit_bytes=63 * 1024 * 1024),
    )(*outs)
    return solution_out[None, None], residual_out[None, None], quadratic[0]


def solution(mesh):
    return jax.shard_map(
        functools.partial(local, mesh.shape["row"], mesh.shape["blk"]),
        mesh=mesh,
        in_specs=(
            P("row", "blk", None, None, None),
            P("row", "blk", None, None),
            P("row", "blk", None, None, None, None),
            P("row", "blk", None, None, None),
            P("row", "blk", None),
            P("row", "blk", None),
            P("row", "blk", None, None, None),
        ),
        out_specs=(P("row", "blk", None, None, None), P("row", "blk", None, None, None), P()),
        check_vma=False,
    )
```

```python
import functools

import jax
import jax.numpy as jnp
from jax import lax
from jax.experimental import pallas as pl
from jax.experimental.pallas import tpu as pltpu
from jax.sharding import PartitionSpec as P

LEAF_ROWS = 2
LEAF_COLS = 4
APPLIES = 4
OWN = 4
MESH = pl.DeviceIdType.MESH
SHIFTS = ((0, -1), (0, 1), (-1, -1), (-1, 1), (1, -1), (1, 1), (-1, 0), (1, 0))
SHIFT_SUM, GRAM_SUM, LAST_SUM = range(3)
SUM_LANES = (128, 256, 384)
EARLY = tuple((i, j) for i in range(APPLIES - 1) for j in range(i + 1))
LATE = tuple((i, j) for i in range(APPLIES - 1, APPLIES + 1) for j in range(i + 1))


def span(shift, count, incoming):
    if shift == 0:
        return 1, count
    if incoming:
        return (0 if shift > 0 else count + 1), 1
    return (count if shift > 0 else 1), 1


def each(count, body):
    if count <= 32:
        for i in range(count):
            body(i)
    else:
        pl.loop(0, count)(body)


def advance(state, gram, shift, count):
    def inner(u, v):
        terms = {}
        for i, a in enumerate(u):
            for j, b in enumerate(v):
                key = (max(i, j), min(i, j))
                terms[key] = a * b + terms[key] if key in terms else a * b
        total = None
        for key, value in terms.items():
            term = value * gram[key]
            total = term if total is None else total + term
        return total

    def apply(u):
        out = [shift * u[0]]
        for j in range(1, len(u)):
            out.append(u[j - 1] + shift * u[j])
        return out + [u[-1]]

    x, r, p, norm = state
    zero = jnp.zeros_like(norm)
    for _ in range(count):
        q = apply(p)
        step = norm / inner(p, q)
        x = [a + step * b for a, b in zip(x + [zero], p)]
        r = [a - step * b for a, b in zip(r + [zero], q)]
        if len(x) < APPLIES:
            norm_next = inner(r, r)
            turn = norm_next / norm
            p = [a + turn * b for a, b in zip(r, p + [zero])]
            norm = norm_next
    return x, r, p, norm


def kernel(
    n_row, n_blk, tracers,
    right_hbm, noise_hbm, blocks_hbm, basis_hbm, index_ref, far_ref, coupling_hbm,
    solution_out, residual_out, quadratic_out,
    vectors, noise_ref, coupling_ref, coupling_twice, blocks, mixed, extended, applied, results, skel_0, skel_1, skel_2, skel_3,
    sum_shift, sum_gram, sum_last, quadratic_ref,
    first_sem, own_sem, load_sem, halo_send, halo_recv, skel_send, skel_recv,
    sum_send, sum_recv, out_sem,
):
    leaves, columns, width = vectors.shape[1:]
    rank = basis_hbm.shape[1]
    far_count = coupling_ref.shape[0]
    my_row, my_blk = lax.axis_index("row"), lax.axis_index("blk")
    skeletons = (skel_0, skel_1, skel_2, skel_3)
    sums_all = (sum_shift, sum_gram, sum_last)
    devices = n_row * n_blk
    me = my_row * n_blk + my_blk
    parity = lax.rem(my_row, 2)
    x_ref, r_ref = results.at[0], results.at[1]

    firsts = [
        pltpu.make_async_copy(source, target, first_sem.at[i])
        for i, (source, target) in enumerate((
            (right_hbm, vectors.at[0]),
            (basis_hbm, mixed.at[:, pl.ds(0, rank)]),
            (noise_hbm, noise_ref),
            (coupling_hbm, coupling_ref),
        ))
    ]
    own_load = pltpu.make_async_copy(blocks_hbm.at[:, OWN], blocks.at[:, OWN], own_sem)
    loads = []
    for l in range(leaves):
        for h, part in enumerate((pl.ds(0, OWN), pl.ds(OWN + 1, 8 - OWN))):
            loads.append(pltpu.make_async_copy(blocks_hbm.at[l, part], blocks.at[l, part], load_sem.at[l, h]))
    firsts[0].start()
    firsts[1].start()
    firsts[2].start()
    own_load.start()
    firsts[3].start()
    for load in loads:
        load.start()

    def row_at(o):
        return lax.rem(my_row + (o + n_row), n_row)

    def blk_at(o):
        return lax.rem(my_blk + (o + n_blk), n_blk)

    barrier = pltpu.get_barrier_semaphore()

    def greet(row, blk):
        pl.semaphore_signal(barrier, inc=1, device_id={"row": row, "blk": blk}, device_id_type=MESH)

    each(devices - 1, lambda i: greet(row_at((i + 1) // n_blk), blk_at((i + 1) % n_blk)))

    def halo(k, n):
        dr, dc = SHIFTS[n]
        (sr, nr), (sc, nc) = span(dr, LEAF_ROWS, False), span(dc, LEAF_COLS, False)
        (tr, _), (tc, _) = span(dr, LEAF_ROWS, True), span(dc, LEAF_COLS, True)
        return pltpu.make_async_remote_copy(
            src_ref=extended.at[k, pl.ds(sr, nr), pl.ds(sc, nc)],
            dst_ref=extended.at[k, pl.ds(tr, nr), pl.ds(tc, nc)],
            send_sem=halo_send.at[k, n],
            recv_sem=halo_recv.at[k, n],
            device_id={"row": row_at(dr), "blk": blk_at(dc)},
            device_id_type=MESH,
        )

    def sum_copy(n, i):
        return pltpu.make_async_remote_copy(
            src_ref=sums_all[n].at[me],
            dst_ref=sums_all[n].at[me],
            send_sem=sum_send.at[n],
            recv_sem=sum_recv.at[n],
            device_id={"row": row_at(i // n_blk), "blk": blk_at(i % n_blk)},
            device_id_type=MESH,
        )

    def skeleton_copy(k, i):
        return pltpu.make_async_remote_copy(
            src_ref=skeletons[k].at[my_blk],
            dst_ref=skeletons[k].at[my_blk],
            send_sem=skel_send.at[k],
            recv_sem=skel_recv.at[k],
            device_id={"row": my_row, "blk": blk_at(i + 1)},
            device_id_type=MESH,
        )

    def all_wait(every, sem):
        pltpu.make_async_copy(every, every, sem).wait()

    def sum_start(n, sums):
        stacked = jnp.concatenate(sums, axis=0)
        rest = SUM_LANES[n] - stacked.shape[0]
        if rest:
            stacked = jnp.concatenate([stacked, jnp.zeros((rest, 128), jnp.float32)], axis=0)
        high = stacked.astype(jnp.bfloat16)
        left = stacked - high.astype(jnp.float32)
        middle = left.astype(jnp.bfloat16)
        low = (left - middle.astype(jnp.float32)).astype(jnp.bfloat16)
        lines = lax.dot_general(
            jnp.ones((8, 3 * 128), jnp.bfloat16), jnp.concatenate([high, middle, low], axis=1),
            (((1,), (1,)), ((), ())), preferred_element_type=jnp.float32,
        )
        sums_all[n][me] = lines[:1]
        each(devices - 1, lambda i: sum_copy(n, devices - 1 - i).start())

    def sum_end(n):
        all_wait(sums_all[n].at[pl.ds(0, devices - 1)], sum_recv.at[n])
        return jnp.sum(sums_all[n][...], axis=0)

    spread_row = lax.broadcasted_iota(jnp.int32, (columns, columns), 0)
    spread_lane = lax.broadcasted_iota(jnp.int32, (columns, columns), 1)

    def per_column(line):
        wide = jnp.broadcast_to(line, (columns, columns))
        kept = jnp.where(spread_row == spread_lane, wide, 0.0)
        return jnp.sum(kept, axis=1, keepdims=True)

    def halves(product):
        total = product[:, :128]
        for h in range(1, width // 128):
            total = total + product[:, 128 * h : 128 * (h + 1)]
        return total

    def at(l):
        a, c = divmod(l, LEAF_COLS)
        return a + 1, c + 1

    def slots(l):
        a, c = divmod(l, LEAF_COLS)
        for s in range(9):
            if s != OWN:
                yield s, a + s // 3, c + s % 3

    def inside(row, col):
        return 1 <= row <= LEAF_ROWS and 1 <= col <= LEAF_COLS

    def publish(k, l, value):
        row, col = at(l)
        extended[k, row, col] = value.astype(jnp.bfloat16)

    def send_halos(k, dc):
        for n, (_, toward) in enumerate(SHIFTS):
            if toward == dc:
                halo(k, n).start()

    def skeleton_part(k, l):
        return lax.dot_general(
            extended[(k, *at(l))], mixed[l], (((1,), (1,)), ((), ())),
            preferred_element_type=jnp.float32,
        )

    def send_skeleton(k, both):
        skeletons[k][my_blk] = (both[:, :rank] + both[:, rank:]).astype(jnp.bfloat16)
        each(n_blk - 1, lambda i: skeleton_copy(k, i).start())

    def own_part(k, l):
        value = vectors[k, l]
        high = extended[(k, *at(l))]
        low = (value - high.astype(jnp.float32)).astype(jnp.bfloat16)
        product = jnp.dot(high, blocks[l, OWN], preferred_element_type=jnp.float32)
        product = product + jnp.dot(low, blocks[l, OWN], preferred_element_type=jnp.float32)
        return noise_ref[l : l + 1] * value + product

    def near_sum(k, l, sources):
        total = None
        for s, row, col in sources:
            term = jnp.dot(extended[k, row, col], blocks[l, s], preferred_element_type=jnp.float32)
            total = term if total is None else total + term
        return total

    def inner_part(k, l):
        return near_sum(k, l, [slot for slot in slots(l) if inside(*slot[1:])])

    def row_part(k, side):
        row = (LEAF_ROWS + 1) * side
        all_wait(extended.at[k, pl.ds(row, 1), pl.ds(1, LEAF_COLS)], halo_recv.at[k, len(SHIFTS) - 1 - side])
        for c in range(LEAF_COLS):
            l = (LEAF_ROWS - 1) * LEAF_COLS * side + c
            sources = [(6 * side + g, row, c + g) for g in range(3) if 1 <= c + g <= LEAF_COLS]
            applied[l] = applied[l] + near_sum(k, l, sources)

    def column_part(k, side):
        for n, (_, toward) in enumerate(SHIFTS):
            if toward == (-1 if side else 1):
                halo(k, n).wait_recv()
        for l in range(leaves):
            edge = (LEAF_COLS + 1) * side
            sources = [slot for slot in slots(l) if slot[2] == edge]
            if sources:
                applied[l] = applied[l] + near_sum(k, l, sources)

    def far_part(k):
        all_wait(skeletons[k].at[pl.ds(0, n_blk - 1)], skel_recv.at[k])
        far = jnp.zeros((columns, 2 * rank), jnp.float32)
        for j in range(far_count):
            far = far + jnp.dot(
                skeletons[k][far_ref[0, j]], coupling_twice[j], preferred_element_type=jnp.float32
            )
        return far.astype(jnp.bfloat16)

    def outer_parts(k):
        row_part(k, 1 - parity)
        row_part(k, parity)
        column_part(k, 0)
        column_part(k, 1)
        far_all = far_part(k)
        return far_all

    def whole(k, l, far_all):
        return applied[l] + jnp.dot(far_all, mixed[l], preferred_element_type=jnp.float32)

    left_edge = [l for l in range(leaves) if l % LEAF_COLS == 0]
    right_edge = [l for l in range(leaves) if l % LEAF_COLS == LEAF_COLS - 1]
    middle = [l for l in range(leaves) if l not in left_edge + right_edge]
    stages = ((left_edge, -1), (right_edge, 1), (middle, 0))

    sublane = lax.broadcasted_iota(jnp.int32, (rank, rank), 0)
    lane = lax.broadcasted_iota(jnp.int32, (rank, rank), 1)
    as_row = jnp.broadcast_to(index_ref[...].astype(jnp.float32), (rank, rank))
    as_column = jnp.sum(jnp.where(sublane == lane, as_row, 0.0), axis=1, keepdims=True)
    point = lax.broadcasted_iota(jnp.int32, (rank, width), 1).astype(jnp.float32)
    for l in range(leaves):
        picks = jnp.where(point + float(width * l) == as_column, 1.0, 0.0).astype(jnp.bfloat16)
        mixed[l, rank:] = picks
    firsts[0].wait()
    for l in range(leaves):
        publish(0, l, vectors[0, l])
    pl.semaphore_wait(barrier, devices - 1)
    for dc in (-1, 1, 0):
        send_halos(0, dc)
    firsts[1].wait()
    send_skeleton(0, sum(skeleton_part(0, l) for l in range(leaves)))
    firsts[2].wait()
    own_load.wait()
    blank = jnp.zeros((columns, 128), jnp.float32)
    sums = {(0, 0): blank}
    curve = blank
    for l in range(leaves):
        value, total = vectors[0, l], own_part(0, l)
        applied[l] = total
        sums[0, 0] = sums[0, 0] + halves(value * value)
        curve = curve + halves(value * total)
    sum_start(SHIFT_SUM, [curve, sums[0, 0]])
    for l in range(leaves):
        loads[2 * l].wait()
        loads[2 * l + 1].wait()
        applied[l] = applied[l] + inner_part(0, l)
    firsts[3].wait()
    for j in range(far_count):
        coupling = coupling_ref[j]
        coupling_twice[j] = jnp.concatenate([coupling, coupling], axis=1)

    def combine(factors, values):
        total = factors[0] * values[0]
        for factor, value in zip(factors[1:], values[1:]):
            total = total + factor * value
        return total

    shift = None
    for k in range(APPLIES):
        far_all = outer_parts(k)
        if k == 0:
            line = sum_end(SHIFT_SUM)
            shift = line[:, :columns] / line[:, columns : 2 * columns]
            shift_c = per_column(shift)
        if k == APPLIES - 1:
            break
        both = jnp.zeros((columns, 2 * rank), jnp.float32)
        for some, dc in stages:
            for l in some:
                total = whole(k, l, far_all) - shift_c * vectors[k, l]
                vectors[k + 1, l] = total
                publish(k + 1, l, total)
                both = both + skeleton_part(k + 1, l)
            if not dc:
                send_skeleton(k + 1, both)
            send_halos(k + 1, dc)
        for j in range(k + 2):
            sums[k + 1, j] = blank
        for l in range(leaves):
            total = vectors[k + 1, l]
            for j in range(k + 2):
                sums[k + 1, j] = sums[k + 1, j] + halves(total * vectors[j, l])
        if k + 1 == APPLIES - 2:
            sum_start(GRAM_SUM, [sums[pair] for pair in EARLY])
        for l in range(leaves):
            applied[l] = own_part(k + 1, l) + inner_part(k + 1, l)

    for j in range(APPLIES + 1):
        sums[APPLIES, j] = blank
    for l in range(leaves):
        total = whole(APPLIES - 1, l, far_all) - shift_c * vectors[APPLIES - 1, l]
        vectors[APPLIES, l] = total
        for j in range(APPLIES + 1):
            sums[APPLIES, j] = sums[APPLIES, j] + halves(total * vectors[j, l])
    sum_start(LAST_SUM, [sums[pair] for pair in LATE])

    def products(line, pairs):
        return {pair: line[:, i * columns : (i + 1) * columns] for i, pair in enumerate(pairs)}

    gram = products(sum_end(GRAM_SUM), EARLY)
    one = jnp.ones((1, columns), jnp.float32)
    state = advance(([], [one], [one], gram[0, 0]), gram, shift, APPLIES - 2)
    gram.update(products(sum_end(LAST_SUM), LATE))
    x, r, _, _ = advance(state, gram, shift, 2)
    x_c, r_c = ([per_column(value) for value in values] for values in (x, r))
    for l in range(leaves):
        values = [vectors[j, l] for j in range(APPLIES + 1)]
        x_ref[l] = combine(x_c, values)
        r_ref[l] = combine(r_c, values)
    quadratic_ref[...] = sum(x[j] * gram[j, 0] for j in range(APPLIES)) * (1.0 / tracers)

    outs = [
        pltpu.make_async_copy(source, target, out_sem.at[i])
        for i, (source, target) in enumerate((
            (x_ref, solution_out), (r_ref, residual_out), (quadratic_ref, quadratic_out),
        ))
    ]
    for out in outs:
        out.start()
    for k in range(APPLIES):
        for n in range(len(SHIFTS)):
            halo(k, n).wait_send()
        all_wait(skeletons[k].at[pl.ds(0, n_blk - 1)], skel_send.at[k])
    for n in range(3):
        all_wait(sums_all[n].at[pl.ds(0, devices - 1)], sum_send.at[n])
    for out in outs:
        out.wait()


def hand_over(
    solution_in, residual_in, quadratic_in, solution_out, residual_out, quadratic_out,
    solution_held, residual_held, quadratic_held, in_sem, out_sem,
):
    held = (solution_held, residual_held, quadratic_held)
    ins = [
        pltpu.make_async_copy(source, slot, in_sem.at[i])
        for i, (source, slot) in enumerate(zip((solution_in, residual_in, quadratic_in), held))
    ]
    outs = [
        pltpu.make_async_copy(slot, target, out_sem.at[i])
        for i, (slot, target) in enumerate(zip(held, (solution_out, residual_out, quadratic_out)))
    ]
    for copy in ins:
        copy.start()
    for copy, out in zip(ins, outs):
        copy.wait()
        out.start()
    for out in outs:
        out.wait()


def local(
    n_row, n_blk,
    right_side, noise_level, near_blocks, skeleton_basis, skeleton_index, far_list, couplings,
):
    leaves, columns, width = right_side.shape[2:]
    rank = skeleton_basis.shape[3]
    field = jax.ShapeDtypeStruct((leaves, columns, width), jnp.float32)
    shapes = (field, field, jax.ShapeDtypeStruct((1, columns), jnp.float32))
    vmem = pl.BlockSpec(memory_space=pltpu.VMEM)
    hbm = pl.BlockSpec(memory_space=pltpu.HBM)
    free = pl.BlockSpec(memory_space=pl.ANY)
    dma = pltpu.SemaphoreType.DMA
    outs = pl.pallas_call(
        functools.partial(kernel, n_row, n_blk, n_row * n_blk * leaves * width),
        out_shape=shapes,
        in_specs=[
            hbm, hbm, hbm, hbm, vmem, pl.BlockSpec(memory_space=pltpu.SMEM), hbm,
        ],
        out_specs=(free, free, free),
        scratch_shapes=[
            pltpu.VMEM((APPLIES + 1, leaves, columns, width), jnp.float32),
            pltpu.VMEM(noise_level.shape[2:], jnp.float32),
            pltpu.VMEM(couplings.shape[2:], jnp.bfloat16),
            pltpu.VMEM((couplings.shape[2], rank, 2 * rank), jnp.bfloat16),
            pltpu.VMEM(near_blocks.shape[2:], jnp.bfloat16),
            pltpu.VMEM((leaves, 2 * rank, width), jnp.bfloat16),
            pltpu.VMEM((APPLIES, LEAF_ROWS + 2, LEAF_COLS + 2, columns, width), jnp.bfloat16),
            pltpu.VMEM((leaves, columns, width), jnp.float32),
            pltpu.VMEM((2, leaves, columns, width), jnp.float32),
            *(pltpu.VMEM((n_blk, columns, rank), jnp.bfloat16) for _ in range(APPLIES)),
            *(pltpu.VMEM((n_row * n_blk, 1, lanes), jnp.float32) for lanes in SUM_LANES),
            pltpu.VMEM((1, columns), jnp.float32),
            dma((4,)), dma, dma((leaves, 2)),
            dma((APPLIES, 8)), dma((APPLIES, 8)),
            dma((APPLIES,)), dma((APPLIES,)),
            dma((3,)), dma((3,)), dma((3,)),
        ],
        compiler_params=pltpu.CompilerParams(
            collective_id=0, has_side_effects=True, vmem_limit_bytes=64512 * 1024
        ),
    )(
        right_side[0, 0], noise_level[0, 0], near_blocks[0, 0], skeleton_basis[0, 0],
        skeleton_index[0], far_list[0], couplings[0, 0],
    )
    solution_out, residual_out, quadratic = pl.pallas_call(
        hand_over,
        out_shape=shapes,
        in_specs=[free, free, free],
        out_specs=(free, free, free),
        scratch_shapes=[*(pltpu.VMEM(shape.shape, shape.dtype) for shape in shapes), dma((3,)), dma((3,))],
        compiler_params=pltpu.CompilerParams(vmem_limit_bytes=63 * 1024 * 1024),
    )(*outs)
    return solution_out[None, None], residual_out[None, None], quadratic[0]


def solution(mesh):
    return jax.shard_map(
        functools.partial(local, mesh.shape["row"], mesh.shape["blk"]),
        mesh=mesh,
        in_specs=(
            P("row", "blk", None, None, None),
            P("row", "blk", None, None),
            P("row", "blk", None, None, None, None),
            P("row", "blk", None, None, None),
            P("row", "blk", None),
            P("row", "blk", None),
            P("row", "blk", None, None, None),
        ),
        out_specs=(P("row", "blk", None, None, None), P("row", "blk", None, None, None), P()),
        check_vma=False,
    )
```

```python
import functools

import jax
import jax.numpy as jnp
from jax import lax
from jax.experimental import pallas as pl
from jax.experimental.pallas import tpu as pltpu
from jax.sharding import PartitionSpec as P

LEAF_ROWS = 2
LEAF_COLS = 4
APPLIES = 4
OWN = 4
MESH = pl.DeviceIdType.MESH
SHIFTS = ((0, -1), (0, 1), (-1, -1), (-1, 1), (1, -1), (1, 1), (-1, 0), (1, 0))
SHIFT_SUM, GRAM_SUM, LAST_SUM = range(3)
SUM_LANES = (128, 256, 384)
EARLY = tuple((i, j) for i in range(APPLIES - 1) for j in range(i + 1))
LATE = tuple((i, j) for i in range(APPLIES - 1, APPLIES + 1) for j in range(i + 1))


def span(shift, count, incoming):
    if shift == 0:
        return 1, count
    if incoming:
        return (0 if shift > 0 else count + 1), 1
    return (count if shift > 0 else 1), 1


def each(count, body):
    if count <= 32:
        for i in range(count):
            body(i)
    else:
        pl.loop(0, count)(body)


def advance(state, gram, shift, count):
    def inner(u, v):
        terms = {}
        for i, a in enumerate(u):
            for j, b in enumerate(v):
                key = (max(i, j), min(i, j))
                terms[key] = a * b + terms[key] if key in terms else a * b
        total = None
        for key, value in terms.items():
            term = value * gram[key]
            total = term if total is None else total + term
        return total

    def apply(u):
        out = [shift * u[0]]
        for j in range(1, len(u)):
            out.append(u[j - 1] + shift * u[j])
        return out + [u[-1]]

    x, r, p, norm = state
    zero = jnp.zeros_like(norm)
    for _ in range(count):
        q = apply(p)
        step = norm / inner(p, q)
        x = [a + step * b for a, b in zip(x + [zero], p)]
        r = [a - step * b for a, b in zip(r + [zero], q)]
        if len(x) < APPLIES:
            norm_next = inner(r, r)
            turn = norm_next / norm
            p = [a + turn * b for a, b in zip(r, p + [zero])]
            norm = norm_next
    return x, r, p, norm


def kernel(
    n_row, n_blk, tracers,
    right_hbm, noise_hbm, blocks_hbm, basis_hbm, index_ref, far_ref, coupling_hbm,
    solution_out, residual_out, quadratic_out,
    vectors, noise_ref, coupling_ref, coupling_twice, blocks, mixed, extended, applied, results, skel_0, skel_1, skel_2, skel_3,
    sum_shift, sum_gram, sum_last, quadratic_ref,
    first_sem, own_sem, load_sem, halo_send, halo_recv, skel_send, skel_recv,
    sum_send, sum_recv, out_sem,
):
    leaves, columns, width = vectors.shape[1:]
    rank = basis_hbm.shape[1]
    far_count = coupling_ref.shape[0]
    my_row, my_blk = lax.axis_index("row"), lax.axis_index("blk")
    skeletons = (skel_0, skel_1, skel_2, skel_3)
    sums_all = (sum_shift, sum_gram, sum_last)
    devices = n_row * n_blk
    me = my_row * n_blk + my_blk
    parity = lax.rem(my_row, 2)
    x_ref, r_ref = results.at[0], results.at[1]

    firsts = [
        pltpu.make_async_copy(source, target, first_sem.at[i])
        for i, (source, target) in enumerate((
            (right_hbm, vectors.at[0]),
            (basis_hbm, mixed.at[:, pl.ds(0, rank)]),
            (noise_hbm, noise_ref),
            (coupling_hbm, coupling_ref),
        ))
    ]
    own_load = pltpu.make_async_copy(blocks_hbm.at[:, OWN], blocks.at[:, OWN], own_sem)
    loads = []
    for l in range(leaves):
        for h, part in enumerate((pl.ds(0, OWN), pl.ds(OWN + 1, 8 - OWN))):
            loads.append(pltpu.make_async_copy(blocks_hbm.at[l, part], blocks.at[l, part], load_sem.at[l, h]))
    firsts[0].start()
    firsts[1].start()
    firsts[2].start()
    own_load.start()
    firsts[3].start()
    for load in loads:
        load.start()

    def row_at(o):
        return lax.rem(my_row + (o + n_row), n_row)

    def blk_at(o):
        return lax.rem(my_blk + (o + n_blk), n_blk)

    barrier = pltpu.get_barrier_semaphore()

    def greet(row, blk):
        pl.semaphore_signal(barrier, inc=1, device_id={"row": row, "blk": blk}, device_id_type=MESH)

    each(devices - 1, lambda i: greet(row_at((i + 1) // n_blk), blk_at((i + 1) % n_blk)))

    def halo(k, n):
        dr, dc = SHIFTS[n]
        (sr, nr), (sc, nc) = span(dr, LEAF_ROWS, False), span(dc, LEAF_COLS, False)
        (tr, _), (tc, _) = span(dr, LEAF_ROWS, True), span(dc, LEAF_COLS, True)
        return pltpu.make_async_remote_copy(
            src_ref=extended.at[k, pl.ds(sr, nr), pl.ds(sc, nc)],
            dst_ref=extended.at[k, pl.ds(tr, nr), pl.ds(tc, nc)],
            send_sem=halo_send.at[k, n],
            recv_sem=halo_recv.at[k, n],
            device_id={"row": row_at(dr), "blk": blk_at(dc)},
            device_id_type=MESH,
        )

    def sum_copy(n, i):
        return pltpu.make_async_remote_copy(
            src_ref=sums_all[n].at[me],
            dst_ref=sums_all[n].at[me],
            send_sem=sum_send.at[n],
            recv_sem=sum_recv.at[n],
            device_id={"row": row_at(i // n_blk), "blk": blk_at(i % n_blk)},
            device_id_type=MESH,
        )

    def skeleton_copy(k, i):
        return pltpu.make_async_remote_copy(
            src_ref=skeletons[k].at[my_blk],
            dst_ref=skeletons[k].at[my_blk],
            send_sem=skel_send.at[k],
            recv_sem=skel_recv.at[k],
            device_id={"row": my_row, "blk": blk_at(i + 1)},
            device_id_type=MESH,
        )

    def all_wait(every, sem):
        pltpu.make_async_copy(every, every, sem).wait()

    def sum_start(n, sums):
        stacked = jnp.concatenate(sums, axis=0)
        rest = SUM_LANES[n] - stacked.shape[0]
        if rest:
            stacked = jnp.concatenate([stacked, jnp.zeros((rest, 128), jnp.float32)], axis=0)
        high = stacked.astype(jnp.bfloat16)
        left = stacked - high.astype(jnp.float32)
        middle = left.astype(jnp.bfloat16)
        low = (left - middle.astype(jnp.float32)).astype(jnp.bfloat16)
        lines = lax.dot_general(
            jnp.ones((8, 3 * 128), jnp.bfloat16), jnp.concatenate([high, middle, low], axis=1),
            (((1,), (1,)), ((), ())), preferred_element_type=jnp.float32,
        )
        sums_all[n][me] = lines[:1]
        each(devices - 1, lambda i: sum_copy(n, devices - 1 - i).start())

    def sum_end(n):
        all_wait(sums_all[n].at[pl.ds(0, devices - 1)], sum_recv.at[n])
        return jnp.sum(sums_all[n][...], axis=0)

    spread_row = lax.broadcasted_iota(jnp.int32, (columns, columns), 0)
    spread_lane = lax.broadcasted_iota(jnp.int32, (columns, columns), 1)

    def per_column(line):
        wide = jnp.broadcast_to(line, (columns, columns))
        kept = jnp.where(spread_row == spread_lane, wide, 0.0)
        return jnp.sum(kept, axis=1, keepdims=True)

    def halves(product):
        total = product[:, :128]
        for h in range(1, width // 128):
            total = total + product[:, 128 * h : 128 * (h + 1)]
        return total

    def at(l):
        a, c = divmod(l, LEAF_COLS)
        return a + 1, c + 1

    def slots(l):
        a, c = divmod(l, LEAF_COLS)
        for s in range(9):
            if s != OWN:
                yield s, a + s // 3, c + s % 3

    def inside(row, col):
        return 1 <= row <= LEAF_ROWS and 1 <= col <= LEAF_COLS

    def publish(k, l, value):
        row, col = at(l)
        extended[k, row, col] = value.astype(jnp.bfloat16)

    def send_halos(k, dc):
        for n, (_, toward) in enumerate(SHIFTS):
            if toward == dc:
                halo(k, n).start()

    def skeleton_part(k, l):
        return lax.dot_general(
            extended[(k, *at(l))], mixed[l], (((1,), (1,)), ((), ())),
            preferred_element_type=jnp.float32,
        )

    def send_skeleton(k, both):
        skeletons[k][my_blk] = (both[:, :rank] + both[:, rank:]).astype(jnp.bfloat16)
        each(n_blk - 1, lambda i: skeleton_copy(k, i).start())

    def own_part(k, l):
        value = vectors[k, l]
        high = extended[(k, *at(l))]
        low = (value - high.astype(jnp.float32)).astype(jnp.bfloat16)
        product = jnp.dot(high, blocks[l, OWN], preferred_element_type=jnp.float32)
        product = product + jnp.dot(low, blocks[l, OWN], preferred_element_type=jnp.float32)
        return noise_ref[l : l + 1] * value + product

    def near_sum(k, l, sources):
        total = None
        for s, row, col in sources:
            term = jnp.dot(extended[k, row, col], blocks[l, s], preferred_element_type=jnp.float32)
            total = term if total is None else total + term
        return total

    def inner_part(k, l):
        return near_sum(k, l, [slot for slot in slots(l) if inside(*slot[1:])])

    def row_part(k, side):
        row = (LEAF_ROWS + 1) * side
        all_wait(extended.at[k, pl.ds(row, 1), pl.ds(1, LEAF_COLS)], halo_recv.at[k, len(SHIFTS) - 1 - side])
        for c in range(LEAF_COLS):
            l = (LEAF_ROWS - 1) * LEAF_COLS * side + c
            sources = [(6 * side + g, row, c + g) for g in range(3) if 1 <= c + g <= LEAF_COLS]
            applied[l] = applied[l] + near_sum(k, l, sources)

    def column_part(k, side):
        for n, (_, toward) in enumerate(SHIFTS):
            if toward == (-1 if side else 1):
                halo(k, n).wait_recv()
        for l in range(leaves):
            edge = (LEAF_COLS + 1) * side
            sources = [slot for slot in slots(l) if slot[2] == edge]
            if sources:
                applied[l] = applied[l] + near_sum(k, l, sources)

    def far_part(k):
        all_wait(skeletons[k].at[pl.ds(0, n_blk - 1)], skel_recv.at[k])
        far = jnp.zeros((columns, 2 * rank), jnp.float32)
        for j in range(far_count):
            far = far + jnp.dot(
                skeletons[k][far_ref[0, j]], coupling_twice[j], preferred_element_type=jnp.float32
            )
        return far.astype(jnp.bfloat16)

    def outer_parts(k):
        row_part(k, 1 - parity)
        row_part(k, parity)
        column_part(k, 0)
        column_part(k, 1)
        far_all = far_part(k)
        return far_all

    def whole(k, l, far_all):
        return applied[l] + jnp.dot(far_all, mixed[l], preferred_element_type=jnp.float32)

    left_edge = [l for l in range(leaves) if l % LEAF_COLS == 0]
    right_edge = [l for l in range(leaves) if l % LEAF_COLS == LEAF_COLS - 1]
    middle = [l for l in range(leaves) if l not in left_edge + right_edge]
    stages = ((left_edge, -1), (right_edge, 1), (middle, 0))

    sublane = lax.broadcasted_iota(jnp.int32, (rank, rank), 0)
    lane = lax.broadcasted_iota(jnp.int32, (rank, rank), 1)
    as_row = jnp.broadcast_to(index_ref[...].astype(jnp.float32), (rank, rank))
    as_column = jnp.sum(jnp.where(sublane == lane, as_row, 0.0), axis=1, keepdims=True)
    point = lax.broadcasted_iota(jnp.int32, (rank, width), 1).astype(jnp.float32)
    for l in range(leaves):
        picks = jnp.where(point + float(width * l) == as_column, 1.0, 0.0).astype(jnp.bfloat16)
        mixed[l, rank:] = picks
    firsts[0].wait()
    for l in range(leaves):
        publish(0, l, vectors[0, l])
    pl.semaphore_wait(barrier, devices - 1)
    for dc in (-1, 1, 0):
        send_halos(0, dc)
    firsts[1].wait()
    send_skeleton(0, sum(skeleton_part(0, l) for l in range(leaves)))
    firsts[2].wait()
    own_load.wait()
    blank = jnp.zeros((columns, 128), jnp.float32)
    sums = {(0, 0): blank}
    curve = blank
    for l in range(leaves):
        value, total = vectors[0, l], own_part(0, l)
        applied[l] = total
        sums[0, 0] = sums[0, 0] + halves(value * value)
        curve = curve + halves(value * total)
    sum_start(SHIFT_SUM, [curve, sums[0, 0]])
    for l in range(leaves):
        loads[2 * l].wait()
        loads[2 * l + 1].wait()
        applied[l] = applied[l] + inner_part(0, l)
    firsts[3].wait()
    for j in range(far_count):
        coupling = coupling_ref[j]
        coupling_twice[j] = jnp.concatenate([coupling, coupling], axis=1)

    def combine(factors, values):
        total = factors[0] * values[0]
        for factor, value in zip(factors[1:], values[1:]):
            total = total + factor * value
        return total

    shift = None
    for k in range(APPLIES):
        far_all = outer_parts(k)
        if k == 0:
            line = sum_end(SHIFT_SUM)
            shift = line[:, :columns] / line[:, columns : 2 * columns]
            shift_c = per_column(shift)
        if k == APPLIES - 1:
            break
        both = jnp.zeros((columns, 2 * rank), jnp.float32)
        for some, dc in stages:
            for l in some:
                total = whole(k, l, far_all) - shift_c * vectors[k, l]
                vectors[k + 1, l] = total
                publish(k + 1, l, total)
                both = both + skeleton_part(k + 1, l)
            if not dc:
                send_skeleton(k + 1, both)
            send_halos(k + 1, dc)
        for j in range(k + 2):
            sums[k + 1, j] = blank
        for l in range(leaves):
            applied[l] = own_part(k + 1, l) + inner_part(k + 1, l)
            total = vectors[k + 1, l]
            for j in range(k + 2):
                sums[k + 1, j] = sums[k + 1, j] + halves(total * vectors[j, l])
        if k + 1 == APPLIES - 2:
            sum_start(GRAM_SUM, [sums[pair] for pair in EARLY])

    for j in range(APPLIES + 1):
        sums[APPLIES, j] = blank
    for l in range(leaves):
        total = whole(APPLIES - 1, l, far_all) - shift_c * vectors[APPLIES - 1, l]
        vectors[APPLIES, l] = total
        for j in range(APPLIES + 1):
            sums[APPLIES, j] = sums[APPLIES, j] + halves(total * vectors[j, l])
    sum_start(LAST_SUM, [sums[pair] for pair in LATE])

    def products(line, pairs):
        return {pair: line[:, i * columns : (i + 1) * columns] for i, pair in enumerate(pairs)}

    gram = products(sum_end(GRAM_SUM), EARLY)
    one = jnp.ones((1, columns), jnp.float32)
    state = advance(([], [one], [one], gram[0, 0]), gram, shift, APPLIES - 2)
    gram.update(products(sum_end(LAST_SUM), LATE))
    x, r, _, _ = advance(state, gram, shift, 2)
    x_c, r_c = ([per_column(value) for value in values] for values in (x, r))
    for l in range(leaves):
        values = [vectors[j, l] for j in range(APPLIES + 1)]
        x_ref[l] = combine(x_c, values)
        r_ref[l] = combine(r_c, values)
    quadratic_ref[...] = sum(x[j] * gram[j, 0] for j in range(APPLIES)) * (1.0 / tracers)

    outs = [
        pltpu.make_async_copy(source, target, out_sem.at[i])
        for i, (source, target) in enumerate((
            (x_ref, solution_out), (r_ref, residual_out), (quadratic_ref, quadratic_out),
        ))
    ]
    for out in outs:
        out.start()
    for k in range(APPLIES):
        for n in range(len(SHIFTS)):
            halo(k, n).wait_send()
        all_wait(skeletons[k].at[pl.ds(0, n_blk - 1)], skel_send.at[k])
    for n in range(3):
        all_wait(sums_all[n].at[pl.ds(0, devices - 1)], sum_send.at[n])
    for out in outs:
        out.wait()


def hand_over(
    solution_in, residual_in, quadratic_in, solution_out, residual_out, quadratic_out,
    solution_held, residual_held, quadratic_held, in_sem, out_sem,
):
    held = (solution_held, residual_held, quadratic_held)
    ins = [
        pltpu.make_async_copy(source, slot, in_sem.at[i])
        for i, (source, slot) in enumerate(zip((solution_in, residual_in, quadratic_in), held))
    ]
    outs = [
        pltpu.make_async_copy(slot, target, out_sem.at[i])
        for i, (slot, target) in enumerate(zip(held, (solution_out, residual_out, quadratic_out)))
    ]
    for copy in ins:
        copy.start()
    for copy, out in zip(ins, outs):
        copy.wait()
        out.start()
    for out in outs:
        out.wait()


def local(
    n_row, n_blk,
    right_side, noise_level, near_blocks, skeleton_basis, skeleton_index, far_list, couplings,
):
    leaves, columns, width = right_side.shape[2:]
    rank = skeleton_basis.shape[3]
    field = jax.ShapeDtypeStruct((leaves, columns, width), jnp.float32)
    shapes = (field, field, jax.ShapeDtypeStruct((1, columns), jnp.float32))
    vmem = pl.BlockSpec(memory_space=pltpu.VMEM)
    hbm = pl.BlockSpec(memory_space=pltpu.HBM)
    free = pl.BlockSpec(memory_space=pl.ANY)
    dma = pltpu.SemaphoreType.DMA
    outs = pl.pallas_call(
        functools.partial(kernel, n_row, n_blk, n_row * n_blk * leaves * width),
        out_shape=shapes,
        in_specs=[
            hbm, hbm, hbm, hbm, vmem, pl.BlockSpec(memory_space=pltpu.SMEM), hbm,
        ],
        out_specs=(free, free, free),
        scratch_shapes=[
            pltpu.VMEM((APPLIES + 1, leaves, columns, width), jnp.float32),
            pltpu.VMEM(noise_level.shape[2:], jnp.float32),
            pltpu.VMEM(couplings.shape[2:], jnp.bfloat16),
            pltpu.VMEM((couplings.shape[2], rank, 2 * rank), jnp.bfloat16),
            pltpu.VMEM(near_blocks.shape[2:], jnp.bfloat16),
            pltpu.VMEM((leaves, 2 * rank, width), jnp.bfloat16),
            pltpu.VMEM((APPLIES, LEAF_ROWS + 2, LEAF_COLS + 2, columns, width), jnp.bfloat16),
            pltpu.VMEM((leaves, columns, width), jnp.float32),
            pltpu.VMEM((2, leaves, columns, width), jnp.float32),
            *(pltpu.VMEM((n_blk, columns, rank), jnp.bfloat16) for _ in range(APPLIES)),
            *(pltpu.VMEM((n_row * n_blk, 1, lanes), jnp.float32) for lanes in SUM_LANES),
            pltpu.VMEM((1, columns), jnp.float32),
            dma((4,)), dma, dma((leaves, 2)),
            dma((APPLIES, 8)), dma((APPLIES, 8)),
            dma((APPLIES,)), dma((APPLIES,)),
            dma((3,)), dma((3,)), dma((3,)),
        ],
        compiler_params=pltpu.CompilerParams(
            collective_id=0, has_side_effects=True, vmem_limit_bytes=64512 * 1024
        ),
    )(
        right_side[0, 0], noise_level[0, 0], near_blocks[0, 0], skeleton_basis[0, 0],
        skeleton_index[0], far_list[0], couplings[0, 0],
    )
    solution_out, residual_out, quadratic = pl.pallas_call(
        hand_over,
        out_shape=shapes,
        in_specs=[free, free, free],
        out_specs=(free, free, free),
        scratch_shapes=[*(pltpu.VMEM(shape.shape, shape.dtype) for shape in shapes), dma((3,)), dma((3,))],
        compiler_params=pltpu.CompilerParams(vmem_limit_bytes=63 * 1024 * 1024),
    )(*outs)
    return solution_out[None, None], residual_out[None, None], quadratic[0]


def solution(mesh):
    return jax.shard_map(
        functools.partial(local, mesh.shape["row"], mesh.shape["blk"]),
        mesh=mesh,
        in_specs=(
            P("row", "blk", None, None, None),
            P("row", "blk", None, None),
            P("row", "blk", None, None, None, None),
            P("row", "blk", None, None, None),
            P("row", "blk", None),
            P("row", "blk", None),
            P("row", "blk", None, None, None),
        ),
        out_specs=(P("row", "blk", None, None, None), P("row", "blk", None, None, None), P()),
        check_vma=False,
    )
```
